32 devices in a mesh: cfg: 2 (over x), work: 16 (over z, y, core).
Axes of the slice: x: 2, y: 2, z: 4, core: 2. Of those that a mesh axis runs over, the one named last changes fastest.
Arguments:
- sources: bfloat16 [32, 16384, 128], P('cfg', 'work'), parts along dimension 0, may hold values from -6 to 6
- perambs: bfloat16 [192, 16384], P('cfg', 'work'), parts along dimension 0, may hold values from -0.5 to 0.5
- source_ids: int32 [16], replicated, may hold values from 0 to 15
- peramb_ids: int32 [48, 3], replicated, may hold values from 0 to 95
- sink_counts: int32 [16], replicated, may hold values from 1 to 6, 48 in all
- weights: float32 [48], replicated, may hold values from -2 to 2, as said below
Outputs:
- sink_tensors: bfloat16 [32, 16384, 128], P(('cfg', 'work')), parts along dimension 0
The draws below stay inside these ranges and needn't reach their ends.
There are 2 independent parts, one for each index of `cfg`. The reference program is written for one: setup_inputs(seed, part) draws one part's arguments, and reference() takes and returns one part's arrays. A program takes and returns all parts, laid end to end along the dimension named above; an argument that names none is the same for every part. Nothing has to cross between parts.
Inputs may be any that keep to these rules, and one draw needn't show every extreme that they name: `sink_counts`: diagrams are listed sink by sink in order; the counts add up to 48 and some sink has exactly 6 diagrams. `weights`: nonzero multiples of 1/4.
All inputs are finite; a program needn't handle non-finite values.
Results may differ from the reference program's by a relative error of at most 0.0064.
Values may be sent and summed in bfloat16 or wider, within the bound.
A program may use at most 128 MiB of HBM per device.

```python
import math
import jax
import jax.numpy as jnp
import numpy as np
from jax import lax

N = 128
MOST = 6
SRC = 16
PERAMB = 96
DIAG = 48
SINK = 16


def draw_weights(key, part):
    key_mag, key_sign = jax.random.split(key)
    magnitude = jax.random.randint(key_mag, (DIAG,), 1, 9).astype(jnp.float32)
    signs = 2.0 * jax.random.randint(key_sign, (DIAG,), 0, 2).astype(jnp.float32) - 1.0
    return magnitude * signs * 0.25


def set_ends(drawn, rng, smallest, top_value):
    shape = drawn.shape
    place = [jax.random.randint(jax.random.fold_in(rng, axis), (), 0, shape[axis]) for axis in range(len(shape))]
    drawn = drawn.at[tuple(place)].set(smallest)
    longest = shape.index(max(shape))
    place[longest] = (place[longest] + 1) % shape[longest]
    return drawn.at[tuple(place)].set(top_value)


def steps_of(stream_key, shape, pieces, low, high):
    def one(position, blocks):
        heights = jax.random.uniform(jax.random.fold_in(jax.random.fold_in(stream_key, 6), position), (blocks,), jnp.float32, low / len(pieces), high / len(pieces))
        return jnp.repeat(jnp.exp(heights), shape[position] // blocks).reshape((-1,) + (1,) * (len(shape) - position - 1))

    level = one(*pieces[0])
    for cut in pieces[1:]:
        level = level * one(*cut)
    return level


def cumulative_ranks(number_of, slope):
    weights = [(1 << 20) // math.isqrt(standing ** slope) + 1 for standing in range(1, number_of + 1)]
    spread = 1 + sum(weights) // (1 << 30)
    return np.cumsum(np.array([max(1, weight // spread) for weight in weights]))


def skewed_ids(own_key, shape, number_of, lean):
    table = cumulative_ranks(number_of, lean)
    lot = jax.random.randint(jax.random.fold_in(own_key, 1), shape, 0, int(table[number_of - 1]))
    standing = jnp.searchsorted(jnp.asarray(table, jnp.int32), lot, side="right")
    return jax.random.permutation(jax.random.fold_in(own_key, 2), number_of)[standing].astype(jnp.int32)


def split_up(count, total, limit, lean):
    weights = [(1 << 20) // math.isqrt(standing ** lean) + 1 for standing in range(2, count + 1)]
    surplus, holding = total - limit - (count - 1), [1] * (count - 1)
    while surplus > 0:
        free = [i for i in range(count - 1) if holding[i] < limit]
        mass, left = sum([weights[i] for i in free]), surplus
        for i in free:
            extra = min(limit - holding[i], max(1, left * weights[i] // mass), surplus)
            holding[i] = holding[i] + extra
            surplus = surplus - extra
    return np.array([limit] + holding)


def uneven(own_key, count, total, bound, lean):
    if count == 2:
        one = jax.random.randint(own_key, (), max(1, total - bound), min(bound, total - 1) + 1)
        return jnp.stack([one, total - one])
    lengths = jnp.asarray(split_up(count, total, bound, lean), jnp.int32)
    twos = (count - 1) // 2
    source_of, sink = lengths[1:1 + 2 * twos:2], lengths[2:2 + 2 * twos:2]
    margin = jnp.minimum(source_of - 1, bound - sink)
    moved = jax.random.randint(jax.random.fold_in(own_key, 1), (twos,), 0, 1 << 20) % (margin + 1)
    lengths = lengths.at[1:1 + 2 * twos:2].set(source_of - moved).at[2:2 + 2 * twos:2].set(sink + moved)
    return lengths[jax.random.permutation(jax.random.fold_in(own_key, 2), count)]


def normal_values(rng, dims, deviation, bound, cuts=(), kind=jnp.bfloat16):
    drawn = jax.random.normal(rng, dims, jnp.float32) * deviation
    if len(cuts) > 0:
        drawn = steps_of(rng, dims, cuts, -0.22, 0.18) * drawn
    return jnp.clip(drawn, min=-bound, max=bound).astype(kind)


def setup_inputs(seed: int = 0, part: int = 0) -> dict:
    keys = jax.random.split(jax.random.key(seed), 7)
    part_splits = jax.random.split(jax.random.fold_in(keys[6], part), 7)
    return {
        "sources": normal_values(part_splits[0], (SRC, N * N, N), 1.0, 6.0, ((1, 16),)),
        "perambs": normal_values(part_splits[1], (PERAMB, N * N), N ** -0.5, 0.5, ((1, 16),)),
        "source_ids": set_ends(skewed_ids(keys[2], (SINK,), SRC, 2), jax.random.fold_in(keys[2], 3), 0, SRC - 1).astype(jnp.int32),
        "peramb_ids": set_ends(jax.random.randint(keys[3], (DIAG, 3), 0, PERAMB), jax.random.fold_in(keys[3], 1), 0, PERAMB - 1).astype(jnp.int32),
        "sink_counts": uneven(keys[4], SINK, DIAG, MOST, 2).astype(jnp.int32),
        "weights": draw_weights(jax.random.fold_in(keys[6], 71), part),
    }


def contract(tensor_rows, leg_mats):
    extent = tensor_rows.shape[1]
    third = jnp.dot(tensor_rows, leg_mats[2].T, preferred_element_type=jnp.float32).astype(jnp.bfloat16)
    third = third.reshape(extent, extent, extent)
    second = jnp.einsum("bk,akc->abc", leg_mats[1].astype(jnp.float32), third.astype(jnp.float32)).astype(jnp.bfloat16)
    whole = jnp.dot(leg_mats[0], second.reshape(extent, extent * extent), preferred_element_type=jnp.float32)
    return whole.reshape(extent * extent, extent)


def reference(sources, perambs, source_ids, peramb_ids, sink_counts, weights):
    matrices = perambs.reshape(PERAMB, N, N)
    sink_ends = jnp.cumsum(sink_counts)
    sink_of = jnp.sum((sink_ends[None, :] <= jnp.arange(DIAG, dtype=jnp.int32)[:, None]).astype(jnp.int32), axis=1)

    def advance(totals, diagram):
        target = sink_of[diagram]
        tensor_rows = sources[source_ids[target]]
        leg_mats = matrices[peramb_ids[diagram]]
        weighted = (weights[diagram] * contract(tensor_rows, leg_mats)).astype(jnp.bfloat16)
        weighted = lax.optimization_barrier(weighted).astype(jnp.float32)
        current = lax.dynamic_index_in_dim(totals, target, 0, keepdims=False)
        totals = lax.dynamic_update_index_in_dim(totals, current + weighted, target, 0)
        return totals, None

    totals, unused = lax.scan(advance, jnp.zeros((SINK, N * N, N), jnp.float32), jnp.arange(DIAG, dtype=jnp.int32))
    return totals.astype(jnp.bfloat16)
```

```python
import functools

import jax
import jax.numpy as jnp
import numpy as np
from jax import lax
from jax.experimental import pallas as pl
from jax.experimental.pallas import tpu as pltpu
from jax.sharding import PartitionSpec as P

MOST = 6
LEGS = 3
PAD = 8
MESH = pl.DeviceIdType.MESH


def plan(workers, own_a):
    half, quarter = workers // 2, workers // 4
    near, mid_j = own_a // 2, own_a // 2
    low_far = half * own_a
    low_late = low_far + quarter * own_a
    last = mid_j + (own_a - mid_j) // 2
    chunks = []

    def add(kind, low, js):
        if len(js) > 0:
            chunks.append((kind, low + quarter * js[0], quarter * len(js), tuple(js)))
            events.append(("work", len(chunks) - 1))

    events = []
    for c in range(2):
        chunks.append(("near", c * half * near, half * near, (c,)))
    events.append(("work", 0))
    events += [("late", j) for j in range(mid_j)]
    events.append(("work", 1))
    events += [("far", j) for j in range(mid_j - 1)]
    add("late", low_late, list(range(mid_j)))
    events += [("far", j) for j in range(mid_j - 1, mid_j + 1)]
    add("far", low_far, list(range(mid_j)))
    events += [("far", j) for j in range(mid_j + 1, own_a)]
    add("far", low_far, list(range(mid_j, own_a)))
    events += [("late", j) for j in range(mid_j, last)]
    add("late", low_late, list(range(mid_j, last)))
    events += [("late", j) for j in range(last, own_a)]
    add("late", low_late, list(range(last, own_a)))

    most = max(count for _, _, count, _ in chunks)
    keys = np.full((2, len(chunks), 1, MOST * most), -1)
    for side in range(2):
        for c, (kind, _, count, js) in enumerate(chunks):
            at = np.arange(count)
            if kind == "near":
                v = side * half + at // near
                j = js[0] * near + at % near
            else:
                sub = 1 - side if kind == "far" else side
                v = (1 - side) * half + sub * quarter + at % quarter
                j = js[0] + at // quarter
            for d in range(MOST):
                keys[side, c, 0, d * count : (d + 1) * count] = d * (workers * own_a) + v * own_a + j
    return chunks, events, most, keys


def contract_kernel(
    workers,
    slots,
    ids_ref,
    pids_ref,
    counts_ref,
    weights_ref,
    key_ref,
    x_hbm,
    p_hbm,
    o_ref,
    xs,
    pv,
    rows,
    xnear,
    xfar,
    lnear,
    lgate,
    lgate_late,
    lfwd,
    xall,
    lbuf,
    fwd,
    legs,
    p1s,
    p2s,
    p3s,
    mid,
    acc,
    stage,
    first_ref,
    rank_ref,
    slot_ref,
    start_ref,
    in_sem,
    lsend,
    lrecv,
    msend,
    mrecv,
    gsend,
    grecv,
    nsend,
    nrecv,
    csend,
    crecv,
    fsend,
    frecv,
    *gates,
):
    own_a, extent = xs.shape[1], xs.shape[3]
    own_rows = lbuf.shape[2]
    diagrams = weights_ref.shape[0]
    half, quarter = workers // 2, workers // 4
    near = own_a // 2
    chunks, events, most, _ = plan(workers, own_a)
    kinds = ("far", "late")
    gate = {"far": gates[:own_a], "late": gates[own_a:]}
    leg_gate = {"far": lgate, "late": lgate_late}
    low_of = {"far": half * own_a, "late": (half + quarter) * own_a}
    step = extent + PAD
    me = lax.axis_index("work")
    side = lax.div(me, half)
    own = lax.rem(me, half)
    lane = lax.rem(me, quarter)
    sub = lax.div(own, quarter)
    base = side * half
    other = (1 - side) * half
    is_gate = sub == 1 - side
    far_gate = lane + quarter * (2 - side)
    owner = {"far": other + (1 - side) * quarter, "late": other + side * quarter}

    p_copy = pltpu.make_async_copy(p_hbm, pv, in_sem.at[0])
    x_copy = pltpu.make_async_copy(x_hbm, xs, in_sem.at[1])
    p_copy.start()
    x_copy.start()

    barrier = pltpu.get_barrier_semaphore()

    def greet(peer):
        pl.semaphore_signal(barrier, inc=1, device_id={"work": peer}, device_id_type=MESH)

    @pl.loop(1, half)
    def _(t):
        greet(base + lax.rem(own + t, half))

    for part in range(2):
        greet(other + part * quarter + lane)

    def tables(low, with_slots):
        def ranked(s, count):
            v = ids_ref[low + s]
            first = lax.fori_loop(
                0,
                half,
                lambda k, m: jnp.minimum(m, jnp.where(ids_ref[low + k] == v, k, half)),
                jnp.int32(half),
                unroll=True,
            )
            is_first = first == s
            first_ref[s] = jnp.where(is_first, count, -1)
            rank_ref[s] = count
            if with_slots:
                slot_ref[s] = rank_ref[first]
            return count + jnp.where(is_first, 1, 0)

        lax.fori_loop(0, half, ranked, jnp.int32(0))

    def start_of(s, start):
        start_ref[s] = start
        return start + counts_ref[s]

    lax.fori_loop(0, workers, start_of, jnp.int32(0))

    def pick_legs(s, source, store):
        for slot in range(MOST):
            d = jnp.minimum(start_ref[base + s] + slot, diagrams - 1)
            for leg in range(LEGS):
                store(slot * LEGS + leg, source[pids_ref[leg, d]])

    def near_leg_copy(t):
        to = lax.rem(own + t, half)
        return pltpu.make_async_remote_copy(
            src_ref=lnear.at[to],
            dst_ref=lbuf.at[me],
            send_sem=lsend.at[t],
            recv_sem=lrecv.at[t],
            device_id={"work": base + to},
            device_id_type=MESH,
        )

    def far_leg_copy(kind):
        return pltpu.make_async_remote_copy(
            src_ref=rows,
            dst_ref=leg_gate[kind],
            send_sem=msend.at[0],
            recv_sem=mrecv.at[kinds.index(kind)],
            device_id={"work": far_gate},
            device_id_type=MESH,
        )

    def pass_leg_copy(kind, t):
        part = kinds.index(kind)
        to = lax.rem(own + t, half)
        return pltpu.make_async_remote_copy(
            src_ref=lfwd.at[part, to],
            dst_ref=lbuf.at[owner[kind] + lane],
            send_sem=gsend.at[part, t],
            recv_sem=grecv.at[part, lane],
            device_id={"work": base + to},
            device_id_type=MESH,
        )

    def leg_arrival(kind, via):
        part = kinds.index(kind)
        return pltpu.make_async_remote_copy(
            src_ref=lfwd.at[part, 0],
            dst_ref=lbuf.at[owner[kind] + via],
            send_sem=gsend.at[part, 0],
            recv_sem=grecv.at[part, via],
            device_id={"work": far_gate},
            device_id_type=MESH,
        )

    def near_copy(c, t):
        to = lax.rem(own + t, half)
        return pltpu.make_async_remote_copy(
            src_ref=xnear.at[to, pl.ds(c * near, near)],
            dst_ref=xall.at[pl.ds((c * half + own) * near, near)],
            send_sem=nsend.at[c, t],
            recv_sem=nrecv.at[c, t],
            device_id={"work": base + to},
            device_id_type=MESH,
        )

    def far_copy(kind, j):
        return pltpu.make_async_remote_copy(
            src_ref=xfar.at[j],
            dst_ref=gate[kind][j],
            send_sem=csend.at[j],
            recv_sem=crecv.at[kinds.index(kind), j],
            device_id={"work": far_gate},
            device_id_type=MESH,
        )

    def pass_copy(kind, j, t):
        part = kinds.index(kind)
        to = lax.rem(own + t, half)
        return pltpu.make_async_remote_copy(
            src_ref=fwd.at[part, j, to],
            dst_ref=xall.at[low_of[kind] + j * quarter + lane],
            send_sem=fsend.at[part, j, t],
            recv_sem=frecv.at[part, j, lane],
            device_id={"work": base + to},
            device_id_type=MESH,
        )

    def arrival(kind, j, via):
        part = kinds.index(kind)
        return pltpu.make_async_remote_copy(
            src_ref=fwd.at[part, j, 0],
            dst_ref=xall.at[low_of[kind] + j * quarter + via],
            send_sem=fsend.at[part, j, 0],
            recv_sem=frecv.at[part, j, via],
            device_id={"work": far_gate},
            device_id_type=MESH,
        )

    def by_role(make):
        pl.when(is_gate)(make("late").start)
        pl.when(jnp.logical_not(is_gate))(make("far").start)

    p_copy.wait()
    for r in range(own_rows):
        rows[:, r, :] = pv[:, r * extent : (r + 1) * extent]
    tables(other, False)

    pl.semaphore_wait(barrier, half + 1)
    by_role(far_leg_copy)

    @pl.loop(0, half)
    def _(s):
        def store(m, value):
            lnear[s, m] = value

        pick_legs(s, rows, store)

    @pl.loop(1, half)
    def _(t):
        near_leg_copy(t).start()

    x_copy.wait()

    @pl.loop(0, half)
    def _(s):
        for j in range(own_a):
            xnear[s, j] = xs[ids_ref[base + s], j]

    for c in range(2):

        @pl.loop(1, half)
        def _(t):
            near_copy(c, t).start()

    @pl.loop(0, slots)
    def _(k):
        source = lax.fori_loop(
            0,
            half,
            lambda s, v: v + jnp.where(first_ref[s] == k, ids_ref[other + s], 0),
            jnp.int32(0),
            unroll=True,
        )
        for j in range(own_a):
            xfar[j, k] = xs[source, j]

    for j in range(own_a):
        by_role(functools.partial(far_copy, j=j))

    lbuf[me] = lnear[own]
    for c in range(2):
        for j in range(near):
            xall[(c * half + own) * near + j] = xnear[own, c * near + j]

    tables(base, True)

    factors = []
    for d in range(MOST):
        value = weights_ref[jnp.minimum(start_ref[me] + d, diagrams - 1)]
        factors.append(jnp.where(d < counts_ref[me], value, 0.0))

    @pl.when(is_gate)
    def _():
        for part, kind in enumerate(kinds):
            far_leg_copy(kind).wait_recv()

            @pl.loop(0, half)
            def _(s):
                def store(m, value):
                    lfwd[part, s, m] = value

                pick_legs(s, leg_gate[kind], store)

            lbuf[owner[kind] + lane] = lfwd[part, own]

            @pl.loop(1, half)
            def _(t):
                pass_leg_copy(kind, t).start()

    def unless_own(via, act):
        pl.when(jnp.logical_not(jnp.logical_and(is_gate, via == lane)))(act)

    @pl.loop(1, half)
    def _(t):
        near_leg_copy(t).wait_recv()

    for kind in kinds:

        @pl.loop(0, quarter)
        def _(via):
            unless_own(via, leg_arrival(kind, via).wait_recv)

    @pl.loop(0, MOST * LEGS)
    def _(m):
        for v in range(workers):
            legs[m, v * own_rows : (v + 1) * own_rows, :] = lbuf[v, m].astype(jnp.float32)

    firsts = []
    for d in range(MOST):
        firsts.append(legs[LEGS * d].astype(jnp.bfloat16))
        p2s[d * extent : (d + 1) * extent, :] = legs[LEGS * d + 1].astype(jnp.bfloat16)
        p3s[d] = legs[LEGS * d + 2].T.astype(jnp.bfloat16)
    wall = jnp.concatenate(firsts, axis=1)
    for c, (_, _, count, _) in enumerate(chunks):
        width = MOST * count
        at = lax.broadcasted_iota(jnp.int32, (MOST * extent, width), 0)
        chosen = jnp.where(at == key_ref[side, c, :, :width], 1.0, 0.0).astype(jnp.bfloat16)
        p1s[c, :, :width] = jnp.dot(wall, chosen, preferred_element_type=jnp.float32).astype(
            jnp.bfloat16
        )

    def forward(kind, j):
        part = kinds.index(kind)

        @pl.when(is_gate)
        def _():
            far_copy(kind, j).wait_recv()

            @pl.loop(0, half)
            def _(s):
                fwd[part, j, s] = gate[kind][j][slot_ref[s]]

            xall[low_of[kind] + j * quarter + lane] = fwd[part, j, own]

            @pl.loop(1, half)
            def _(t):
                pass_copy(kind, j, t).start()

    group = 4
    wide = 8

    def work(c):
        kind, low, count, js = chunks[c]
        if kind == "near":

            @pl.loop(1, half)
            def _(t):
                near_copy(js[0], t).wait_recv()

        else:
            for j in js:

                @pl.loop(0, quarter)
                def _(via):
                    unless_own(via, arrival(kind, j, via).wait_recv)

        @pl.loop(0, count // group, unroll=2)
        def _(g):
            both = jnp.concatenate([xall[low + g * group + i] for i in range(group)], axis=1)
            for d in range(MOST):
                z = jnp.dot(
                    p2s[d * extent : (d + 1) * extent, :], both, preferred_element_type=jnp.float32
                ).astype(jnp.bfloat16)
                stacked = jnp.concatenate(
                    [z[:, i * extent : (i + 1) * extent] for i in range(group)], axis=0
                )
                y = jnp.dot(stacked, p3s[d], preferred_element_type=jnp.float32) * factors[d]
                for i in range(group):
                    at = pl.multiple_of((d * count + group * g + i) * step, 8)
                    mid[pl.ds(at, extent), :] = y[i * extent : (i + 1) * extent]

        def pieces(b):
            cols = [
                mid[pl.ds(wide * b + h, MOST * count, stride=step), :].astype(jnp.bfloat16)
                for h in range(wide)
            ]
            t = jnp.dot(
                p1s[c, :, : MOST * count],
                jnp.concatenate(cols, axis=1),
                preferred_element_type=jnp.float32,
            )
            out = []
            for h in range(wide):
                at = pl.ds(pl.multiple_of((wide * b + h) * extent, 8), extent)
                piece = t[:, h * extent : (h + 1) * extent]
                out.append((at, piece if c == 0 else piece + acc[at, :]))
            return out

        if c < len(chunks) - 1:

            @pl.loop(0, extent // wide)
            def _(b):
                for at, piece in pieces(b):
                    acc[at, :] = piece

        else:

            @pl.loop(0, extent // (2 * wide))
            def _(b):
                for part in range(2):
                    for h, (at, piece) in enumerate(pieces(2 * b + part)):
                        stage[:, part * wide + h, :] = piece
                at = pl.ds(pl.multiple_of(2 * wide * b, 2 * wide), 2 * wide)
                o_ref[:, at, :] = stage[:, : 2 * wide, :].astype(jnp.bfloat16)

    for what, at in events:
        if what == "work":
            work(at)
        else:
            forward(what, at)

    @pl.loop(1, half)
    def _(t):
        near_leg_copy(t).wait_send()

    far_leg_copy("far").wait_send()
    for c in range(2):

        @pl.loop(1, half)
        def _(t):
            near_copy(c, t).wait_send()

    for j in range(own_a):
        far_copy("far", j).wait_send()

    @pl.when(is_gate)
    def _():
        for kind in kinds:

            @pl.loop(1, half)
            def _(t):
                pass_leg_copy(kind, t).wait_send()

            for j in range(own_a):

                @pl.loop(1, half)
                def _(t):
                    pass_copy(kind, j, t).wait_send()


def contract(x, perambs, ids, pids, counts, weights, workers, slots):
    own_a, extent = x.shape[1], x.shape[2]
    own_rows = own_a
    half, quarter = workers // 2, workers // 4
    chunks, _, most, keys = plan(workers, own_a)
    step = extent + PAD
    smem = pl.BlockSpec(memory_space=pltpu.SMEM)
    hbm = pl.BlockSpec(memory_space=pltpu.HBM)
    slab = (extent, extent)
    bf16, f32 = jnp.bfloat16, jnp.float32
    legs = MOST * LEGS
    pieces = (perambs.shape[0], own_rows, extent)
    dma = pltpu.SemaphoreType.DMA
    return pl.pallas_call(
        functools.partial(contract_kernel, workers, slots),
        out_shape=jax.ShapeDtypeStruct((extent, extent, extent), bf16),
        in_specs=[smem, smem, smem, smem, pl.BlockSpec(memory_space=pltpu.VMEM), hbm, hbm],
        out_specs=pl.BlockSpec(memory_space=pltpu.VMEM),
        scratch_shapes=[
            pltpu.VMEM(x.shape, bf16),
            pltpu.VMEM(perambs.shape, bf16),
            pltpu.VMEM(pieces, bf16),
            pltpu.VMEM((half, own_a) + slab, bf16),
            pltpu.VMEM((own_a, slots) + slab, bf16),
            pltpu.VMEM((half, legs, own_rows, extent), bf16),
            pltpu.VMEM(pieces, bf16),
            pltpu.VMEM(pieces, bf16),
            pltpu.VMEM((2, half, legs, own_rows, extent), bf16),
            pltpu.VMEM((workers * own_a,) + slab, bf16),
            pltpu.VMEM((workers, legs, own_rows, extent), bf16),
            pltpu.VMEM((2, own_a, half) + slab, bf16),
            pltpu.VMEM((legs,) + slab, f32),
            pltpu.VMEM((len(chunks), extent, MOST * most), bf16),
            pltpu.VMEM((MOST * extent, extent), bf16),
            pltpu.VMEM((MOST,) + slab, bf16),
            pltpu.VMEM((MOST * most * step, extent), f32),
            pltpu.VMEM((extent * extent, extent), f32),
            pltpu.VMEM((extent, 24, extent), f32),
            pltpu.SMEM((half,), jnp.int32),
            pltpu.SMEM((half,), jnp.int32),
            pltpu.SMEM((half,), jnp.int32),
            pltpu.SMEM((workers,), jnp.int32),
            dma((2,)),
            dma((half,)),
            dma((half,)),
            dma((1,)),
            dma((2,)),
            dma((2, half)),
            dma((2, quarter)),
            dma((2, half)),
            dma((2, half)),
            dma((own_a,)),
            dma((2, own_a)),
            dma((2, own_a, half)),
            dma((2, own_a, quarter)),
        ]
        + [pltpu.VMEM((slots,) + slab, bf16) for _ in range(2 * own_a)],
        compiler_params=pltpu.CompilerParams(
            vmem_limit_bytes=54 * 1024 * 1024, collective_id=0, has_side_effects=True
        ),
        name="contract",
    )(ids, pids, counts, weights, jnp.asarray(keys, jnp.int32), x, perambs)


def per_device(sources, perambs, source_ids, peramb_ids, sink_counts, weights):
    workers = lax.axis_size("work")
    extent = sources.shape[2]
    own_a = sources.shape[1] // extent
    x = sources.reshape(-1, own_a, extent, extent)
    total = contract(
        x, perambs, source_ids, peramb_ids.T, sink_counts, weights, workers, workers // 2
    )
    return total.reshape(1, extent * extent, extent)


def solution(mesh):
    return jax.shard_map(
        per_device,
        mesh=mesh,
        in_specs=(P("cfg", "work", None), P("cfg", "work"), P(), P(), P(), P()),
        out_specs=P(("cfg", "work"), None, None),
        check_vma=False,
    )
```

```python
import functools

import jax
import jax.numpy as jnp
import numpy as np
from jax import lax
from jax.experimental import pallas as pl
from jax.experimental.pallas import tpu as pltpu
from jax.sharding import PartitionSpec as P

MOST = 6
LEGS = 3
PAD = 8
GROUP = 4
WIDE = 8
MESH = pl.DeviceIdType.MESH


def plan(workers, own_a, slots):
    half, quarter = workers // 2, workers // 4
    near = own_a // 2
    size = half * near
    early = max(0, min(own_a - 2, int(quarter * own_a / slots - 0.75)))
    items = [("late", j) for j in range(early)]
    items += [("far", j) for j in range(own_a)]
    items += [("late", j) for j in range(early, own_a)]
    tail = max(1, 8 // quarter)
    body = len(items) - tail

    slabs = []
    for c in range(2):
        slabs += [(("near", v), c * near + j) for v in range(half) for j in range(near)]
    for kind, j in items:
        slabs += [((kind, v), j) for v in range(quarter)]
    split = 2 * size + body * quarter
    groups = [slabs[low : min(low + size, split)] for low in range(0, split, size)]
    groups.append(slabs[split:])
    keys = np.full((2, len(groups), 1, MOST * size), -1)
    for side in range(2):
        first = {
            "near": side * half,
            "far": (1 - side) * half + (1 - side) * quarter,
            "late": (1 - side) * half + side * quarter,
        }
        for g, group in enumerate(groups):
            stride = size if g < len(groups) - 1 else len(group)
            for at, ((kind, v), j) in enumerate(group):
                for d in range(MOST):
                    a = (first[kind] + v) * own_a + j
                    keys[side, g, 0, d * stride + at] = d * (workers * own_a) + a

    unit = GROUP
    near_steps, item_steps = size // unit, quarter // unit
    begin = 2 * near_steps
    when = []
    for f in range(len(items)):
        if f < 3:
            at = (0, near_steps - 1, near_steps)[f]
        elif f == 3 and early > 3:
            at = begin - 1
        elif f < body:
            at = begin + item_steps * (f - 2)
        elif f < len(items) - 1:
            at = begin + item_steps * (f - 1)
        else:
            at = begin + item_steps * body
        when.append(min(at, begin + item_steps * f))
    return items, early, size, len(groups), body, when, keys


def contract_kernel(
    workers,
    slots,
    ids_ref,
    pids_ref,
    counts_ref,
    weights_ref,
    key_ref,
    x_hbm,
    p_hbm,
    o_ref,
    xs,
    pv,
    rows,
    xnear,
    xfar,
    lnear,
    lgate,
    lgate_late,
    lfwd,
    xall,
    lbuf,
    fwd,
    legs,
    p1s,
    p2s,
    p3s,
    mid,
    acc,
    stage,
    first_ref,
    rank_ref,
    slot_ref,
    start_ref,
    in_sem,
    lsend,
    lrecv,
    msend,
    mrecv,
    gsend,
    grecv,
    nsend,
    nrecv,
    csend,
    crecv,
    fsend,
    frecv,
    *gates,
):
    own_a, extent = xs.shape[1], xs.shape[3]
    own_rows = lbuf.shape[2]
    diagrams = weights_ref.shape[0]
    half, quarter = workers // 2, workers // 4
    near = own_a // 2
    items, early, size, groups, main, when, _ = plan(workers, own_a, slots)
    kinds = ("far", "late")
    gate = {"far": gates[:own_a], "late": gates[own_a:]}
    leg_gate = {"far": lgate, "late": lgate_late}
    low_of = {"far": half * own_a, "late": (half + quarter) * own_a}
    step = extent + PAD
    me = lax.axis_index("work")
    side = lax.div(me, half)
    own = lax.rem(me, half)
    lane = lax.rem(me, quarter)
    sub = lax.div(own, quarter)
    base = side * half
    other = (1 - side) * half
    is_gate = sub == 1 - side
    far_gate = lane + quarter * (2 - side)
    owner = {"far": other + (1 - side) * quarter, "late": other + side * quarter}

    p_copy = pltpu.make_async_copy(p_hbm, pv, in_sem.at[0])
    x_copy = pltpu.make_async_copy(x_hbm, xs, in_sem.at[1])
    p_copy.start()
    x_copy.start()

    barrier = pltpu.get_barrier_semaphore()

    def greet(peer):
        pl.semaphore_signal(barrier, inc=1, device_id={"work": peer}, device_id_type=MESH)

    @pl.loop(1, half)
    def _(t):
        greet(base + lax.rem(own + t, half))

    for part in range(2):
        greet(other + part * quarter + lane)

    def tables(low, with_slots):
        def ranked(s, count):
            v = ids_ref[low + s]
            first = lax.fori_loop(
                0,
                half,
                lambda k, m: jnp.minimum(m, jnp.where(ids_ref[low + k] == v, k, half)),
                jnp.int32(half),
                unroll=True,
            )
            is_first = first == s
            first_ref[s] = jnp.where(is_first, count, -1)
            rank_ref[s] = count
            if with_slots:
                slot_ref[s] = rank_ref[first]
            return count + jnp.where(is_first, 1, 0)

        lax.fori_loop(0, half, ranked, jnp.int32(0))

    def start_of(s, start):
        start_ref[s] = start
        return start + counts_ref[s]

    lax.fori_loop(0, workers, start_of, jnp.int32(0))

    def pick_legs(s, source, store):
        for slot in range(MOST):
            d = jnp.minimum(start_ref[base + s] + slot, diagrams - 1)
            for leg in range(LEGS):
                store(slot * LEGS + leg, source[pids_ref[leg, d]])

    def near_leg_copy(t):
        to = lax.rem(own + t, half)
        return pltpu.make_async_remote_copy(
            src_ref=lnear.at[to],
            dst_ref=lbuf.at[me],
            send_sem=lsend.at[t],
            recv_sem=lrecv.at[t],
            device_id={"work": base + to},
            device_id_type=MESH,
        )

    def far_leg_copy(kind):
        return pltpu.make_async_remote_copy(
            src_ref=rows,
            dst_ref=leg_gate[kind],
            send_sem=msend.at[0],
            recv_sem=mrecv.at[kinds.index(kind)],
            device_id={"work": far_gate},
            device_id_type=MESH,
        )

    def pass_leg_copy(kind, t):
        part = kinds.index(kind)
        to = lax.rem(own + t, half)
        return pltpu.make_async_remote_copy(
            src_ref=lfwd.at[part, to],
            dst_ref=lbuf.at[owner[kind] + lane],
            send_sem=gsend.at[part, t],
            recv_sem=grecv.at[part, lane],
            device_id={"work": base + to},
            device_id_type=MESH,
        )

    def leg_arrival(kind, via):
        part = kinds.index(kind)
        return pltpu.make_async_remote_copy(
            src_ref=lfwd.at[part, 0],
            dst_ref=lbuf.at[owner[kind] + via],
            send_sem=gsend.at[part, 0],
            recv_sem=grecv.at[part, via],
            device_id={"work": far_gate},
            device_id_type=MESH,
        )

    def near_copy(c, t):
        to = lax.rem(own + t, half)
        return pltpu.make_async_remote_copy(
            src_ref=xnear.at[to, pl.ds(c * near, near)],
            dst_ref=xall.at[pl.ds((c * half + own) * near, near)],
            send_sem=nsend.at[c, t],
            recv_sem=nrecv.at[c, t],
            device_id={"work": base + to},
            device_id_type=MESH,
        )

    def far_copy(kind, j):
        return pltpu.make_async_remote_copy(
            src_ref=xfar.at[j],
            dst_ref=gate[kind][j],
            send_sem=csend.at[j],
            recv_sem=crecv.at[kinds.index(kind), j],
            device_id={"work": far_gate},
            device_id_type=MESH,
        )

    def pass_copy(kind, j, t):
        part = kinds.index(kind)
        to = lax.rem(own + t, half)
        return pltpu.make_async_remote_copy(
            src_ref=fwd.at[part, j, to],
            dst_ref=xall.at[low_of[kind] + j * quarter + lane],
            send_sem=fsend.at[part, j, t],
            recv_sem=frecv.at[part, j, lane],
            device_id={"work": base + to},
            device_id_type=MESH,
        )

    def by_role(make):
        pl.when(is_gate)(make("late").start)
        pl.when(jnp.logical_not(is_gate))(make("far").start)

    p_copy.wait()
    for r in range(own_rows):
        rows[:, r, :] = pv[:, r * extent : (r + 1) * extent]
    tables(other, False)

    pl.semaphore_wait(barrier, half + 1)
    by_role(far_leg_copy)

    @pl.loop(0, half)
    def _(s):
        def store(m, value):
            lnear[s, m] = value

        pick_legs(s, rows, store)

    @pl.loop(1, half)
    def _(t):
        near_leg_copy(t).start()

    x_copy.wait()

    @pl.loop(0, half)
    def _(s):
        for j in range(own_a):
            xnear[s, j] = xs[ids_ref[base + s], j]

    def start_near(c):
        @pl.loop(1, half)
        def _(t):
            near_copy(c, t).start()

    start_near(0)
    pl.when(jnp.logical_not(is_gate))(lambda: start_near(1))

    @pl.loop(0, slots)
    def _(k):
        source = lax.fori_loop(
            0,
            half,
            lambda s, v: v + jnp.where(first_ref[s] == k, ids_ref[other + s], 0),
            jnp.int32(0),
            unroll=True,
        )
        for j in range(own_a):
            xfar[j, k] = xs[source, j]

    for j in range(own_a):
        by_role(functools.partial(far_copy, j=j))

    @pl.when(is_gate)
    def _():
        for part, kind in enumerate(kinds):
            far_leg_copy(kind).wait_recv()

            @pl.loop(0, half)
            def _(s):
                def store(m, value):
                    lfwd[part, s, m] = value

                pick_legs(s, leg_gate[kind], store)

            lbuf[owner[kind] + lane] = lfwd[part, own]

            @pl.loop(1, half)
            def _(t):
                pass_leg_copy(kind, t).start()

        start_near(1)

    tables(base, True)

    @pl.loop(0, extent)
    def _(b):
        acc[pl.ds(pl.multiple_of(b * extent, extent), extent), :] = jnp.zeros(
            (extent, extent), jnp.float32
        )

    lbuf[me] = lnear[own]
    for c in range(2):
        for j in range(near):
            xall[(c * half + own) * near + j] = xnear[own, c * near + j]

    factors = []
    for d in range(MOST):
        value = weights_ref[jnp.minimum(start_ref[me] + d, diagrams - 1)]
        factors.append(jnp.where(d < counts_ref[me], value, 0.0))

    def unless_own(via, act):
        pl.when(jnp.logical_not(jnp.logical_and(is_gate, via == lane)))(act)

    @pl.loop(1, half)
    def _(t):
        near_leg_copy(t).wait_recv()

    for kind in kinds:

        @pl.loop(0, quarter)
        def _(via):
            unless_own(via, leg_arrival(kind, via).wait_recv)

    @pl.loop(0, MOST * LEGS)
    def _(m):
        for v in range(workers):
            legs[m, v * own_rows : (v + 1) * own_rows, :] = lbuf[v, m].astype(jnp.float32)

    firsts = []
    for d in range(MOST):
        firsts.append(legs[LEGS * d].astype(jnp.bfloat16))
        p2s[d * extent : (d + 1) * extent, :] = legs[LEGS * d + 1].astype(jnp.bfloat16)
        p3s[d] = legs[LEGS * d + 2].T.astype(jnp.bfloat16)
    wall = jnp.concatenate(firsts, axis=1)
    width = MOST * size
    at = lax.broadcasted_iota(jnp.int32, (MOST * extent, width), 0)
    for g in range(groups):
        chosen = jnp.where(at == key_ref[side, g], 1.0, 0.0).astype(jnp.bfloat16)
        p1s[g] = jnp.dot(wall, chosen, preferred_element_type=jnp.float32).astype(jnp.bfloat16)

    def forward(kind, j):
        part = kinds.index(kind)

        @pl.when(is_gate)
        def _():
            far_copy(kind, j).wait_recv()

            @pl.loop(0, half)
            def _(s):
                fwd[part, j, s] = gate[kind][j][slot_ref[s]]

            xall[low_of[kind] + j * quarter + lane] = fwd[part, j, own]

            @pl.loop(1, half)
            def _(t):
                pass_copy(kind, j, t).start()

    near_steps, item_steps = size // GROUP, quarter // GROUP
    begin = 2 * near_steps
    main_steps = begin + item_steps * main
    last_steps = item_steps * (len(items) - main)
    last = last_steps * GROUP

    def reached(value, limit):
        span = 2 * workers * own_a
        return lax.div(value - limit + span, span)

    def pieces(b, columns, count):
        cols = [
            mid[pl.ds(WIDE * b + h, MOST * count, stride=step), :].astype(jnp.bfloat16)
            for h in range(WIDE)
        ]
        t = jnp.dot(columns, jnp.concatenate(cols, axis=1), preferred_element_type=jnp.float32)
        out = []
        for h in range(WIDE):
            at = pl.ds(pl.multiple_of((WIDE * b + h) * extent, 8), extent)
            out.append((at, t[:, h * extent : (h + 1) * extent] + acc[at, :]))
        return out

    @pl.loop(0, main_steps + last_steps)
    def _(st):
        for f, (kind, j) in enumerate(items):
            pl.when(st == when[f])(functools.partial(forward, kind, j))

        for c in range(2):

            @pl.when(st == c * near_steps)
            def _():
                @pl.loop(1, half)
                def _(t):
                    near_copy(c, t).wait_recv()

        past = reached(st, begin)
        i = lax.div(past * (st - begin), item_steps)
        inside = lax.rem(past * (st - begin), item_steps)
        middle, end = reached(i, early), reached(i, early + own_a)
        part = 1 - middle + end
        j = i - middle * early - end * (own_a - early)
        low = half * own_a + (part * own_a + j) * quarter

        @pl.when(jnp.logical_and(past == 1, inside == 0))
        def _():
            @pl.loop(0, quarter)
            def _(via):
                @pl.when(jnp.logical_not(jnp.logical_and(is_gate, via == lane)))
                def _():
                    pltpu.make_async_remote_copy(
                        src_ref=fwd.at[part, j, 0],
                        dst_ref=xall.at[low + via],
                        send_sem=fsend.at[part, j, 0],
                        recv_sem=frecv.at[part, j, via],
                        device_id={"work": far_gate},
                        device_id_type=MESH,
                    ).wait_recv()

        x_at = (1 - past) * st * GROUP + past * (low + inside * GROUP)
        final = reached(st, main_steps)
        stride = size + final * (last - size)
        start = ((1 - final) * lax.rem(st, near_steps) + final * (st - main_steps)) * GROUP
        both = jnp.concatenate([xall[x_at + n] for n in range(GROUP)], axis=1)
        for d in range(MOST):
            z = jnp.dot(
                p2s[d * extent : (d + 1) * extent, :], both, preferred_element_type=jnp.float32
            ).astype(jnp.bfloat16)
            stacked = jnp.concatenate(
                [z[:, n * extent : (n + 1) * extent] for n in range(GROUP)], axis=0
            )
            y = jnp.dot(stacked, p3s[d], preferred_element_type=jnp.float32) * factors[d]
            for n in range(GROUP):
                at = pl.multiple_of((d * stride + start + n) * step, 8)
                mid[pl.ds(at, extent), :] = y[n * extent : (n + 1) * extent]

        full = jnp.logical_and(st < main_steps, lax.rem(st, near_steps) == near_steps - 1)

        @pl.when(jnp.logical_or(full, st == main_steps - 1))
        def _():
            g = lax.div(st, near_steps)

            @pl.loop(0, extent // WIDE)
            def _(b):
                for at, piece in pieces(b, p1s[g], size):
                    acc[at, :] = piece

    @pl.loop(0, extent // (2 * WIDE))
    def _(b):
        for part in range(2):
            for h, (at, piece) in enumerate(
                pieces(2 * b + part, p1s[groups - 1, :, : MOST * last], last)
            ):
                stage[:, part * WIDE + h, :] = piece
        at = pl.ds(pl.multiple_of(2 * WIDE * b, 2 * WIDE), 2 * WIDE)
        o_ref[:, at, :] = stage[:, : 2 * WIDE, :].astype(jnp.bfloat16)

    @pl.loop(1, half)
    def _(t):
        near_leg_copy(t).wait_send()

    far_leg_copy("far").wait_send()
    for c in range(2):

        @pl.loop(1, half)
        def _(t):
            near_copy(c, t).wait_send()

    for j in range(own_a):
        far_copy("far", j).wait_send()

    @pl.when(is_gate)
    def _():
        for kind in kinds:

            @pl.loop(1, half)
            def _(t):
                pass_leg_copy(kind, t).wait_send()

            for j in range(own_a):

                @pl.loop(1, half)
                def _(t):
                    pass_copy(kind, j, t).wait_send()


def contract(x, perambs, ids, pids, counts, weights, *, workers, slots, number):
    own_a, extent = x.shape[1], x.shape[2]
    own_rows = own_a
    half, quarter = workers // 2, workers // 4
    _, _, size, groups, _, _, keys = plan(workers, own_a, slots)
    step = extent + PAD
    smem = pl.BlockSpec(memory_space=pltpu.SMEM)
    hbm = pl.BlockSpec(memory_space=pltpu.HBM)
    slab = (extent, extent)
    bf16, f32 = jnp.bfloat16, jnp.float32
    legs = MOST * LEGS
    pieces = (perambs.shape[0], own_rows, extent)
    dma = pltpu.SemaphoreType.DMA
    return pl.pallas_call(
        functools.partial(contract_kernel, workers, slots),
        out_shape=jax.ShapeDtypeStruct((extent, extent, extent), bf16),
        in_specs=[smem, smem, smem, smem, pl.BlockSpec(memory_space=pltpu.VMEM), hbm, hbm],
        out_specs=pl.BlockSpec(memory_space=pltpu.VMEM),
        scratch_shapes=[
            pltpu.VMEM(x.shape, bf16),
            pltpu.VMEM(perambs.shape, bf16),
            pltpu.VMEM(pieces, bf16),
            pltpu.VMEM((half, own_a) + slab, bf16),
            pltpu.VMEM((own_a, slots) + slab, bf16),
            pltpu.VMEM((half, legs, own_rows, extent), bf16),
            pltpu.VMEM(pieces, bf16),
            pltpu.VMEM(pieces, bf16),
            pltpu.VMEM((2, half, legs, own_rows, extent), bf16),
            pltpu.VMEM((workers * own_a,) + slab, bf16),
            pltpu.VMEM((workers, legs, own_rows, extent), bf16),
            pltpu.VMEM((2, own_a, half) + slab, bf16),
            pltpu.VMEM((legs,) + slab, f32),
            pltpu.VMEM((groups, extent, MOST * size), bf16),
            pltpu.VMEM((MOST * extent, extent), bf16),
            pltpu.VMEM((MOST,) + slab, bf16),
            pltpu.VMEM((MOST * size * step, extent), f32),
            pltpu.VMEM((extent * extent, extent), f32),
            pltpu.VMEM((extent, 24, extent), f32),
            pltpu.SMEM((half,), jnp.int32),
            pltpu.SMEM((half,), jnp.int32),
            pltpu.SMEM((half,), jnp.int32),
            pltpu.SMEM((workers,), jnp.int32),
            dma((2,)),
            dma((half,)),
            dma((half,)),
            dma((1,)),
            dma((2,)),
            dma((2, half)),
            dma((2, quarter)),
            dma((2, half)),
            dma((2, half)),
            dma((own_a,)),
            dma((2, own_a)),
            dma((2, own_a, half)),
            dma((2, own_a, quarter)),
        ]
        + [pltpu.VMEM((slots,) + slab, bf16) for _ in range(2 * own_a)],
        compiler_params=pltpu.CompilerParams(
            vmem_limit_bytes=48 * 1024 * 1024, collective_id=number, has_side_effects=True
        ),
        name=f"contract_{slots}",
    )(ids, pids, counts, weights, jnp.asarray(keys, jnp.int32), x, perambs)


def per_device(sources, perambs, source_ids, peramb_ids, sink_counts, weights):
    workers = lax.axis_size("work")
    extent = sources.shape[2]
    own_a = sources.shape[1] // extent
    x = sources.reshape(-1, own_a, extent, extent)
    half = workers // 2
    caps = sorted({-(-half * part // 8) for part in (6, 7, 8)})
    groups = source_ids.reshape(2, half)
    before = np.tril(np.ones((half, half), bool), -1)
    same = groups[:, :, None] == groups[:, None, :]
    repeats = jnp.sum(jnp.any(same & before, axis=2).astype(jnp.int32), axis=1)
    most = half - jnp.min(repeats)
    which = sum((most > cap).astype(jnp.int32) for cap in caps[:-1])
    total = lax.switch(
        which,
        [
            functools.partial(contract, workers=workers, slots=cap, number=i)
            for i, cap in enumerate(caps)
        ],
        x,
        perambs,
        source_ids,
        peramb_ids.T,
        sink_counts,
        weights,
    )
    return total.reshape(1, extent * extent, extent)


def solution(mesh):
    return jax.shard_map(
        per_device,
        mesh=mesh,
        in_specs=(P("cfg", "work", None), P("cfg", "work"), P(), P(), P(), P()),
        out_specs=P(("cfg", "work"), None, None),
        check_vma=False,
    )
```

```python
import functools

import jax
import jax.numpy as jnp
import numpy as np
from jax import lax
from jax.experimental import pallas as pl
from jax.experimental.pallas import tpu as pltpu
from jax.sharding import PartitionSpec as P

MOST = 6
LEGS = 3
PAD = 8
GROUP = 4
WIDE = 8
MESH = pl.DeviceIdType.MESH


def plan(workers, own_a, slots):
    half, quarter = workers // 2, workers // 4
    near = own_a // 2
    size = half * near
    early = max(0, min(own_a - 2, int(quarter * own_a / slots - 0.75)))
    items = [("late", j) for j in range(early)]
    items += [("far", j) for j in range(own_a)]
    items += [("late", j) for j in range(early, own_a)]
    tail = max(1, 8 // quarter)
    body = len(items) - tail

    slabs = []
    for c in range(2):
        slabs += [(("near", v), c * near + j) for v in range(half) for j in range(near)]
    for kind, j in items:
        slabs += [((kind, v), j) for v in range(quarter)]
    split = 2 * size + body * quarter
    groups = [slabs[low : min(low + size, split)] for low in range(0, split, size)]
    groups.append(slabs[split:])
    keys = np.full((2, len(groups), 1, MOST * size), -1)
    for side in range(2):
        first = {
            "near": side * half,
            "far": (1 - side) * half + (1 - side) * quarter,
            "late": (1 - side) * half + side * quarter,
        }
        for g, group in enumerate(groups):
            stride = size if g < len(groups) - 1 else len(group)
            for at, ((kind, v), j) in enumerate(group):
                for d in range(MOST):
                    a = (first[kind] + v) * own_a + j
                    keys[side, g, 0, d * stride + at] = d * (workers * own_a) + a

    unit = GROUP
    near_steps, item_steps = size // unit, quarter // unit
    begin = 2 * near_steps
    when = []
    for f in range(len(items)):
        if f < 3:
            at = (0, near_steps - 1, near_steps)[f]
        elif f == 3 and early > 3:
            at = begin - 1
        elif f < body:
            at = begin + item_steps * (f - 2)
        elif f < len(items) - 1:
            at = begin + item_steps * (f - 1)
        else:
            at = begin + item_steps * body
        when.append(min(at, begin + item_steps * f))
    return items, early, size, len(groups), body, when, keys


def contract_kernel(
    workers,
    slots,
    ids_ref,
    pids_ref,
    counts_ref,
    weights_ref,
    key_ref,
    x_hbm,
    p_hbm,
    o_ref,
    xs,
    pv,
    rows,
    xnear,
    xfar,
    lnear,
    lgate,
    lgate_late,
    lfwd,
    xall,
    lbuf,
    fwd,
    legs,
    p1s,
    p2s,
    p3s,
    mid,
    acc,
    stage,
    first_ref,
    rank_ref,
    slot_ref,
    start_ref,
    in_sem,
    lsend,
    lrecv,
    msend,
    mrecv,
    gsend,
    grecv,
    nsend,
    nrecv,
    csend,
    crecv,
    fsend,
    frecv,
    *gates,
):
    own_a, extent = xs.shape[1], xs.shape[3]
    own_rows = lbuf.shape[2]
    diagrams = weights_ref.shape[0]
    half, quarter = workers // 2, workers // 4
    near = own_a // 2
    items, early, size, groups, main, when, _ = plan(workers, own_a, slots)
    kinds = ("far", "late")
    gate = {"far": gates[:own_a], "late": gates[own_a:]}
    leg_gate = {"far": lgate, "late": lgate_late}
    low_of = {"far": half * own_a, "late": (half + quarter) * own_a}
    step = extent + PAD
    me = lax.axis_index("work")
    side = lax.div(me, half)
    own = lax.rem(me, half)
    lane = lax.rem(me, quarter)
    sub = lax.div(own, quarter)
    base = side * half
    other = (1 - side) * half
    is_gate = sub == 1 - side
    far_gate = lane + quarter * (2 - side)
    owner = {"far": other + (1 - side) * quarter, "late": other + side * quarter}

    p_copy = pltpu.make_async_copy(p_hbm, pv, in_sem.at[0])
    x_copy = pltpu.make_async_copy(x_hbm, xs, in_sem.at[1])
    p_copy.start()
    x_copy.start()

    barrier = pltpu.get_barrier_semaphore()

    def greet(peer):
        pl.semaphore_signal(barrier, inc=1, device_id={"work": peer}, device_id_type=MESH)

    @pl.loop(1, half)
    def _(t):
        greet(base + lax.rem(own + t, half))

    for part in range(2):
        greet(other + part * quarter + lane)

    def tables(low, with_slots):
        def ranked(s, count):
            v = ids_ref[low + s]
            first = lax.fori_loop(
                0,
                half,
                lambda k, m: jnp.minimum(m, jnp.where(ids_ref[low + k] == v, k, half)),
                jnp.int32(half),
                unroll=True,
            )
            is_first = first == s
            first_ref[s] = jnp.where(is_first, count, -1)
            rank_ref[s] = count
            if with_slots:
                slot_ref[s] = rank_ref[first]
            return count + jnp.where(is_first, 1, 0)

        lax.fori_loop(0, half, ranked, jnp.int32(0))

    def start_of(s, start):
        start_ref[s] = start
        return start + counts_ref[s]

    lax.fori_loop(0, workers, start_of, jnp.int32(0))

    def pick_legs(s, source, store):
        for slot in range(MOST):
            d = jnp.minimum(start_ref[base + s] + slot, diagrams - 1)
            for leg in range(LEGS):
                store(slot * LEGS + leg, source[pids_ref[leg, d]])

    def near_leg_copy(t):
        to = lax.rem(own + t, half)
        return pltpu.make_async_remote_copy(
            src_ref=lnear.at[to],
            dst_ref=lbuf.at[me],
            send_sem=lsend.at[0],
            recv_sem=lrecv.at[0],
            device_id={"work": base + to},
            device_id_type=MESH,
        )

    def far_leg_copy(kind):
        return pltpu.make_async_remote_copy(
            src_ref=rows,
            dst_ref=leg_gate[kind],
            send_sem=msend.at[0],
            recv_sem=mrecv.at[kinds.index(kind)],
            device_id={"work": far_gate},
            device_id_type=MESH,
        )

    def pass_leg_copy(kind, t):
        part = kinds.index(kind)
        to = lax.rem(own + t, half)
        return pltpu.make_async_remote_copy(
            src_ref=lfwd.at[part, to],
            dst_ref=lbuf.at[owner[kind] + lane],
            send_sem=gsend.at[0],
            recv_sem=grecv.at[0],
            device_id={"work": base + to},
            device_id_type=MESH,
        )

    def take(ref, sem):
        pltpu.make_async_copy(ref, ref, sem).wait()

    def take_lanes(ref_of, sem):
        pl.when(is_gate)(lambda: take(ref_of(quarter - 1), sem))
        pl.when(jnp.logical_not(is_gate))(lambda: take(ref_of(quarter), sem))

    def near_copy(c, t):
        to = lax.rem(own + t, half)
        return pltpu.make_async_remote_copy(
            src_ref=xnear.at[to, pl.ds(c * near, near)],
            dst_ref=xall.at[pl.ds((c * half + own) * near, near)],
            send_sem=nsend.at[0],
            recv_sem=nrecv.at[c],
            device_id={"work": base + to},
            device_id_type=MESH,
        )

    def far_copy(kind, j):
        return pltpu.make_async_remote_copy(
            src_ref=xfar.at[j],
            dst_ref=gate[kind][j],
            send_sem=csend.at[0],
            recv_sem=crecv.at[kinds.index(kind), j],
            device_id={"work": far_gate},
            device_id_type=MESH,
        )

    def pass_copy(kind, j, t):
        part = kinds.index(kind)
        to = lax.rem(own + t, half)
        return pltpu.make_async_remote_copy(
            src_ref=fwd.at[part, j, to],
            dst_ref=xall.at[low_of[kind] + j * quarter + lane],
            send_sem=fsend.at[0],
            recv_sem=frecv.at[part, j],
            device_id={"work": base + to},
            device_id_type=MESH,
        )

    def by_role(make):
        pl.when(is_gate)(make("late").start)
        pl.when(jnp.logical_not(is_gate))(make("far").start)

    p_copy.wait()
    for r in range(own_rows):
        rows[:, r, :] = pv[:, r * extent : (r + 1) * extent]
    tables(other, False)

    pl.semaphore_wait(barrier, half + 1)
    by_role(far_leg_copy)

    @pl.loop(0, half)
    def _(s):
        def store(m, value):
            lnear[s, m] = value

        pick_legs(s, rows, store)

    @pl.loop(1, half)
    def _(t):
        near_leg_copy(t).start()

    x_copy.wait()

    @pl.loop(0, half)
    def _(s):
        for j in range(own_a):
            xnear[s, j] = xs[ids_ref[base + s], j]

    def start_near(c):
        @pl.loop(1, half)
        def _(t):
            near_copy(c, t).start()

    start_near(0)
    pl.when(jnp.logical_not(is_gate))(lambda: start_near(1))

    @pl.loop(0, slots)
    def _(k):
        source = lax.fori_loop(
            0,
            half,
            lambda s, v: v + jnp.where(first_ref[s] == k, ids_ref[other + s], 0),
            jnp.int32(0),
            unroll=True,
        )
        for j in range(own_a):
            xfar[j, k] = xs[source, j]

    for j in range(own_a):
        by_role(functools.partial(far_copy, j=j))

    @pl.when(is_gate)
    def _():
        for part, kind in enumerate(kinds):
            far_leg_copy(kind).wait_recv()

            @pl.loop(0, half)
            def _(s):
                def store(m, value):
                    lfwd[part, s, m] = value

                pick_legs(s, leg_gate[kind], store)

            lbuf[owner[kind] + lane] = lfwd[part, own]

            @pl.loop(1, half)
            def _(t):
                pass_leg_copy(kind, t).start()

        start_near(1)

    tables(base, True)

    @pl.loop(0, extent)
    def _(b):
        acc[pl.ds(pl.multiple_of(b * extent, extent), extent), :] = jnp.zeros(
            (extent, extent), jnp.float32
        )

    lbuf[me] = lnear[own]
    for c in range(2):
        for j in range(near):
            xall[(c * half + own) * near + j] = xnear[own, c * near + j]

    factors = []
    for d in range(MOST):
        value = weights_ref[jnp.minimum(start_ref[me] + d, diagrams - 1)]
        factors.append(jnp.where(d < counts_ref[me], value, 0.0))

    lbuf[me] = lnear[own]
    for c in range(2):
        for j in range(near):
            xall[(c * half + own) * near + j] = xnear[own, c * near + j]

    factors = []
    for d in range(MOST):
        value = weights_ref[jnp.minimum(start_ref[me] + d, diagrams - 1)]
        factors.append(jnp.where(d < counts_ref[me], value, 0.0))

    take(lbuf.at[pl.ds(0, half - 1)], lrecv.at[0])
    take_lanes(lambda lanes: lbuf.at[pl.ds(0, 2 * lanes)], grecv.at[0])

    @pl.loop(0, MOST * LEGS)
    def _(m):
        for v in range(workers):
            legs[m, v * own_rows : (v + 1) * own_rows, :] = lbuf[v, m].astype(jnp.float32)

    firsts = []
    for d in range(MOST):
        firsts.append(legs[LEGS * d].astype(jnp.bfloat16))
        p2s[d * extent : (d + 1) * extent, :] = legs[LEGS * d + 1].astype(jnp.bfloat16)
        p3s[d] = legs[LEGS * d + 2].T.astype(jnp.bfloat16)
    wall = jnp.concatenate(firsts, axis=1)
    width = MOST * size
    at = lax.broadcasted_iota(jnp.int32, (MOST * extent, width), 0)
    for g in range(groups):
        chosen = jnp.where(at == key_ref[side, g], 1.0, 0.0).astype(jnp.bfloat16)
        p1s[g] = jnp.dot(wall, chosen, preferred_element_type=jnp.float32).astype(jnp.bfloat16)

    def forward(kind, j):
        part = kinds.index(kind)

        @pl.when(is_gate)
        def _():
            far_copy(kind, j).wait_recv()

            @pl.loop(0, half)
            def _(s):
                fwd[part, j, s] = gate[kind][j][slot_ref[s]]

            xall[low_of[kind] + j * quarter + lane] = fwd[part, j, own]

            @pl.loop(1, half)
            def _(t):
                pass_copy(kind, j, t).start()

    near_steps, item_steps = size // GROUP, quarter // GROUP
    begin = 2 * near_steps
    main_steps = begin + item_steps * main
    last_steps = item_steps * (len(items) - main)
    last = last_steps * GROUP

    def reached(value, limit):
        span = 2 * workers * own_a
        return lax.div(value - limit + span, span)

    def pieces(b, columns, count):
        cols = [
            mid[pl.ds(WIDE * b + h, MOST * count, stride=step), :].astype(jnp.bfloat16)
            for h in range(WIDE)
        ]
        t = jnp.dot(columns, jnp.concatenate(cols, axis=1), preferred_element_type=jnp.float32)
        out = []
        for h in range(WIDE):
            at = pl.ds(pl.multiple_of((WIDE * b + h) * extent, 8), extent)
            out.append((at, t[:, h * extent : (h + 1) * extent] + acc[at, :]))
        return out

    @pl.loop(0, main_steps + last_steps)
    def _(st):
        for f, (kind, j) in enumerate(items):
            pl.when(st == when[f])(functools.partial(forward, kind, j))

        for c in range(2):

            @pl.when(st == c * near_steps)
            def _():
                take(xall.at[pl.ds(0, (half - 1) * near)], nrecv.at[c])

        past = reached(st, begin)
        i = lax.div(past * (st - begin), item_steps)
        inside = lax.rem(past * (st - begin), item_steps)
        middle, end = reached(i, early), reached(i, early + own_a)
        part = 1 - middle + end
        j = i - middle * early - end * (own_a - early)
        low = half * own_a + (part * own_a + j) * quarter

        @pl.when(jnp.logical_and(past == 1, inside == 0))
        def _():
            take_lanes(lambda lanes: xall.at[pl.ds(0, lanes)], frecv.at[part, j])

        x_at = (1 - past) * st * GROUP + past * (low + inside * GROUP)
        final = reached(st, main_steps)
        stride = size + final * (last - size)
        start = ((1 - final) * lax.rem(st, near_steps) + final * (st - main_steps)) * GROUP
        both = jnp.concatenate([xall[x_at + n] for n in range(GROUP)], axis=1)
        for d in range(MOST):
            z = jnp.dot(
                p2s[d * extent : (d + 1) * extent, :], both, preferred_element_type=jnp.float32
            ).astype(jnp.bfloat16)
            stacked = jnp.concatenate(
                [z[:, n * extent : (n + 1) * extent] for n in range(GROUP)], axis=0
            )
            y = jnp.dot(stacked, p3s[d], preferred_element_type=jnp.float32) * factors[d]
            for n in range(GROUP):
                at = pl.multiple_of((d * stride + start + n) * step, 8)
                mid[pl.ds(at, extent), :] = y[n * extent : (n + 1) * extent]

        full = jnp.logical_and(st < main_steps, lax.rem(st, near_steps) == near_steps - 1)

        @pl.when(jnp.logical_or(full, st == main_steps - 1))
        def _():
            g = lax.div(st, near_steps)

            @pl.loop(0, extent // WIDE)
            def _(b):
                for at, piece in pieces(b, p1s[g], size):
                    acc[at, :] = piece

    @pl.loop(0, extent // (2 * WIDE))
    def _(b):
        for part in range(2):
            for h, (at, piece) in enumerate(
                pieces(2 * b + part, p1s[groups - 1, :, : MOST * last], last)
            ):
                stage[:, part * WIDE + h, :] = piece
        at = pl.ds(pl.multiple_of(2 * WIDE * b, 2 * WIDE), 2 * WIDE)
        o_ref[:, at, :] = stage[:, : 2 * WIDE, :].astype(jnp.bfloat16)

    take(lnear.at[pl.ds(0, half - 1)], lsend.at[0])
    far_leg_copy("far").wait_send()
    take(xnear.at[pl.ds(0, half - 1)], nsend.at[0])
    take(xfar, csend.at[0])

    @pl.when(is_gate)
    def _():
        take(lfwd.at[:, pl.ds(0, half - 1)], gsend.at[0])
        take(fwd.at[:, :, pl.ds(0, half - 1)], fsend.at[0])


def contract(x, perambs, ids, pids, counts, weights, *, workers, slots, number):
    own_a, extent = x.shape[1], x.shape[2]
    own_rows = own_a
    half, quarter = workers // 2, workers // 4
    _, _, size, groups, _, _, keys = plan(workers, own_a, slots)
    step = extent + PAD
    smem = pl.BlockSpec(memory_space=pltpu.SMEM)
    hbm = pl.BlockSpec(memory_space=pltpu.HBM)
    slab = (extent, extent)
    bf16, f32 = jnp.bfloat16, jnp.float32
    legs = MOST * LEGS
    pieces = (perambs.shape[0], own_rows, extent)
    dma = pltpu.SemaphoreType.DMA
    return pl.pallas_call(
        functools.partial(contract_kernel, workers, slots),
        out_shape=jax.ShapeDtypeStruct((extent, extent, extent), bf16),
        in_specs=[smem, smem, smem, smem, pl.BlockSpec(memory_space=pltpu.VMEM), hbm, hbm],
        out_specs=pl.BlockSpec(memory_space=pltpu.VMEM),
        scratch_shapes=[
            pltpu.VMEM(x.shape, bf16),
            pltpu.VMEM(perambs.shape, bf16),
            pltpu.VMEM(pieces, bf16),
            pltpu.VMEM((half, own_a) + slab, bf16),
            pltpu.VMEM((own_a, slots) + slab, bf16),
            pltpu.VMEM((half, legs, own_rows, extent), bf16),
            pltpu.VMEM(pieces, bf16),
            pltpu.VMEM(pieces, bf16),
            pltpu.VMEM((2, half, legs, own_rows, extent), bf16),
            pltpu.VMEM((workers * own_a,) + slab, bf16),
            pltpu.VMEM((workers, legs, own_rows, extent), bf16),
            pltpu.VMEM((2, own_a, half) + slab, bf16),
            pltpu.VMEM((legs,) + slab, f32),
            pltpu.VMEM((groups, extent, MOST * size), bf16),
            pltpu.VMEM((MOST * extent, extent), bf16),
            pltpu.VMEM((MOST,) + slab, bf16),
            pltpu.VMEM((MOST * size * step, extent), f32),
            pltpu.VMEM((extent * extent, extent), f32),
            pltpu.VMEM((extent, 24, extent), f32),
            pltpu.SMEM((half,), jnp.int32),
            pltpu.SMEM((half,), jnp.int32),
            pltpu.SMEM((half,), jnp.int32),
            pltpu.SMEM((workers,), jnp.int32),
            dma((2,)),
            dma((1,)),
            dma((1,)),
            dma((1,)),
            dma((2,)),
            dma((1,)),
            dma((1,)),
            dma((1,)),
            dma((2,)),
            dma((1,)),
            dma((2, own_a)),
            dma((1,)),
            dma((2, own_a)),
        ]
        + [pltpu.VMEM((slots,) + slab, bf16) for _ in range(2 * own_a)],
        compiler_params=pltpu.CompilerParams(
            vmem_limit_bytes=48 * 1024 * 1024, collective_id=number, has_side_effects=True
        ),
        name=f"contract_{slots}",
    )(ids, pids, counts, weights, jnp.asarray(keys, jnp.int32), x, perambs)


def choose_kernel(caps, ids_ref, o_ref):
    half = ids_ref.shape[0] // 2

    def distinct(low):
        def one(s, count):
            v = ids_ref[low + s]
            seen = lax.fori_loop(
                0,
                half,
                lambda k, m: m + jnp.where(jnp.logical_and(k < s, ids_ref[low + k] == v), 1, 0),
                jnp.int32(0),
                unroll=True,
            )
            return count + jnp.where(seen == 0, 1, 0)

        return lax.fori_loop(0, half, one, jnp.int32(0), unroll=half <= 8)

    most = jnp.maximum(distinct(0), distinct(half))
    which = jnp.int32(0)
    for cap in caps[:-1]:
        which = which + jnp.where(most > cap, 1, 0)
    o_ref[0] = which


def choose(ids, caps):
    smem = pl.BlockSpec(memory_space=pltpu.SMEM)
    return pl.pallas_call(
        functools.partial(choose_kernel, caps),
        out_shape=jax.ShapeDtypeStruct((1,), jnp.int32),
        in_specs=[smem],
        out_specs=smem,
        name="choose",
    )(ids)[0]


def per_device(sources, perambs, source_ids, peramb_ids, sink_counts, weights):
    workers = lax.axis_size("work")
    extent = sources.shape[2]
    own_a = sources.shape[1] // extent
    x = sources.reshape(-1, own_a, extent, extent)
    half = workers // 2
    caps = sorted({-(-half * part // 8) for part in (6, 7, 8)})
    which = choose(source_ids, caps)
    total = lax.switch(
        which,
        [
            functools.partial(contract, workers=workers, slots=cap, number=i)
            for i, cap in enumerate(caps)
        ],
        x,
        perambs,
        source_ids,
        peramb_ids.T,
        sink_counts,
        weights,
    )
    return total.reshape(1, extent * extent, extent)


def solution(mesh):
    return jax.shard_map(
        per_device,
        mesh=mesh,
        in_specs=(P("cfg", "work", None), P("cfg", "work"), P(), P(), P(), P()),
        out_specs=P(("cfg", "work"), None, None),
        check_vma=False,
    )
```

```python
import functools

import jax
import jax.numpy as jnp
import numpy as np
from jax import lax
from jax.experimental import pallas as pl
from jax.experimental.pallas import tpu as pltpu
from jax.sharding import PartitionSpec as P

MOST = 6
LEGS = 3
PAD = 8
GROUP = 4
WIDE = 8
MESH = pl.DeviceIdType.MESH


def plan(workers, own_a, slots):
    half, quarter = workers // 2, workers // 4
    near = own_a // 2
    size = half * near
    early = max(0, min(own_a - 2, int(quarter * own_a / slots - 0.75)))
    items = [("late", j) for j in range(early)]
    items += [("far", j) for j in range(own_a)]
    items += [("late", j) for j in range(early, own_a)]
    tail = max(1, 8 // quarter)
    body = len(items) - tail

    slabs = []
    for c in range(2):
        slabs += [(("near", v), c * near + j) for v in range(half) for j in range(near)]
    for kind, j in items:
        slabs += [((kind, v), j) for v in range(quarter)]
    split = 2 * size + body * quarter
    groups = [slabs[low : min(low + size, split)] for low in range(0, split, size)]
    groups.append(slabs[split:])
    keys = np.full((2, len(groups), 1, MOST * size), -1)
    for side in range(2):
        first = {
            "near": side * half,
            "far": (1 - side) * half + (1 - side) * quarter,
            "late": (1 - side) * half + side * quarter,
        }
        for g, group in enumerate(groups):
            stride = size if g < len(groups) - 1 else len(group)
            for at, ((kind, v), j) in enumerate(group):
                for d in range(MOST):
                    a = (first[kind] + v) * own_a + j
                    keys[side, g, 0, d * stride + at] = d * (workers * own_a) + a

    unit = GROUP
    near_steps, item_steps = size // unit, quarter // unit
    begin = 2 * near_steps
    when = []
    for f in range(len(items)):
        if f < 3:
            at = (0, near_steps - 1, near_steps)[f]
        elif f == 3 and early > 3:
            at = begin - 1
        elif f < body:
            at = begin + item_steps * (f - 2)
        elif f < len(items) - 1:
            at = begin + item_steps * (f - 1)
        else:
            at = begin + item_steps * body
        when.append(min(at, begin + item_steps * f))
    return items, early, size, len(groups), body, when, keys


def contract_kernel(
    workers,
    slots,
    ids_ref,
    pids_ref,
    counts_ref,
    weights_ref,
    key_ref,
    x_hbm,
    p_hbm,
    o_ref,
    xs,
    pv,
    rows,
    xnear,
    xfar,
    lnear,
    lgate,
    lgate_late,
    lfwd,
    xall,
    lbuf,
    fwd,
    legs,
    p1s,
    p2s,
    p3s,
    mid,
    acc,
    stage,
    first_ref,
    rank_ref,
    slot_ref,
    start_ref,
    in_sem,
    lsend,
    lrecv,
    msend,
    mrecv,
    gsend,
    grecv,
    nsend,
    nrecv,
    csend,
    crecv,
    fsend,
    frecv,
    *gates,
):
    own_a, extent = xs.shape[1], xs.shape[3]
    own_rows = lbuf.shape[2]
    diagrams = weights_ref.shape[0]
    half, quarter = workers // 2, workers // 4
    near = own_a // 2
    items, early, size, groups, main, when, _ = plan(workers, own_a, slots)
    kinds = ("far", "late")
    gate = {"far": gates[:own_a], "late": gates[own_a:]}
    leg_gate = {"far": lgate, "late": lgate_late}
    low_of = {"far": half * own_a, "late": (half + quarter) * own_a}
    step = extent + PAD
    me = lax.axis_index("work")
    side = lax.div(me, half)
    own = lax.rem(me, half)
    lane = lax.rem(me, quarter)
    sub = lax.div(own, quarter)
    base = side * half
    other = (1 - side) * half
    is_gate = sub == 1 - side
    far_gate = lane + quarter * (2 - side)
    owner = {"far": other + (1 - side) * quarter, "late": other + side * quarter}

    p_copy = pltpu.make_async_copy(p_hbm, pv, in_sem.at[0])
    x_copy = pltpu.make_async_copy(x_hbm, xs, in_sem.at[1])
    p_copy.start()
    x_copy.start()

    barrier = pltpu.get_barrier_semaphore()

    def greet(peer):
        pl.semaphore_signal(barrier, inc=1, device_id={"work": peer}, device_id_type=MESH)

    @pl.loop(1, half)
    def _(t):
        greet(base + lax.rem(own + t, half))

    for part in range(2):
        greet(other + part * quarter + lane)

    def tables(low, with_slots):
        def ranked(s, count):
            v = ids_ref[low + s]
            first = lax.fori_loop(
                0,
                half,
                lambda k, m: jnp.minimum(m, jnp.where(ids_ref[low + k] == v, k, half)),
                jnp.int32(half),
                unroll=True,
            )
            is_first = first == s
            first_ref[s] = jnp.where(is_first, count, -1)
            rank_ref[s] = count
            if with_slots:
                slot_ref[s] = rank_ref[first]
            return count + jnp.where(is_first, 1, 0)

        lax.fori_loop(0, half, ranked, jnp.int32(0))

    def start_of(s, start):
        start_ref[s] = start
        return start + counts_ref[s]

    lax.fori_loop(0, workers, start_of, jnp.int32(0))

    def pick_legs(s, source, store):
        for slot in range(MOST):
            d = jnp.minimum(start_ref[base + s] + slot, diagrams - 1)
            for leg in range(LEGS):
                store(slot * LEGS + leg, source[pids_ref[leg, d]])

    def near_leg_copy(t):
        to = lax.rem(own + t, half)
        return pltpu.make_async_remote_copy(
            src_ref=lnear.at[to],
            dst_ref=lbuf.at[me],
            send_sem=lsend.at[0],
            recv_sem=lrecv.at[0],
            device_id={"work": base + to},
            device_id_type=MESH,
        )

    def far_leg_copy(kind):
        return pltpu.make_async_remote_copy(
            src_ref=rows,
            dst_ref=leg_gate[kind],
            send_sem=msend.at[0],
            recv_sem=mrecv.at[kinds.index(kind)],
            device_id={"work": far_gate},
            device_id_type=MESH,
        )

    def pass_leg_copy(kind, t):
        part = kinds.index(kind)
        to = lax.rem(own + t, half)
        return pltpu.make_async_remote_copy(
            src_ref=lfwd.at[part, to],
            dst_ref=lbuf.at[owner[kind] + lane],
            send_sem=gsend.at[0],
            recv_sem=grecv.at[0],
            device_id={"work": base + to},
            device_id_type=MESH,
        )

    def take(ref, sem):
        pltpu.make_async_copy(ref, ref, sem).wait()

    def take_lanes(ref_of, sem):
        pl.when(is_gate)(lambda: take(ref_of(quarter - 1), sem))
        pl.when(jnp.logical_not(is_gate))(lambda: take(ref_of(quarter), sem))

    def near_copy(c, t):
        to = lax.rem(own + t, half)
        return pltpu.make_async_remote_copy(
            src_ref=xnear.at[to, pl.ds(c * near, near)],
            dst_ref=xall.at[pl.ds((c * half + own) * near, near)],
            send_sem=nsend.at[0],
            recv_sem=nrecv.at[c],
            device_id={"work": base + to},
            device_id_type=MESH,
        )

    def far_copy(kind, j):
        return pltpu.make_async_remote_copy(
            src_ref=xfar.at[j],
            dst_ref=gate[kind][j],
            send_sem=csend.at[0],
            recv_sem=crecv.at[kinds.index(kind), j],
            device_id={"work": far_gate},
            device_id_type=MESH,
        )

    def pass_copy(kind, j, t):
        part = kinds.index(kind)
        to = lax.rem(own + t, half)
        return pltpu.make_async_remote_copy(
            src_ref=fwd.at[part, j, to],
            dst_ref=xall.at[low_of[kind] + j * quarter + lane],
            send_sem=fsend.at[0],
            recv_sem=frecv.at[part, j],
            device_id={"work": base + to},
            device_id_type=MESH,
        )

    def by_role(make):
        pl.when(is_gate)(make("late").start)
        pl.when(jnp.logical_not(is_gate))(make("far").start)

    p_copy.wait()
    total = rows.shape[0]
    if own_rows % 8 == 0 and total * own_rows <= legs.shape[0]:
        for r in range(own_rows):
            piece = pv[:, r * extent : (r + 1) * extent].astype(jnp.float32)
            legs[pl.ds(r, total, stride=own_rows), :] = piece
        whole = legs[: total * own_rows, :].reshape(total, own_rows, extent)
        rows[...] = whole.astype(jnp.bfloat16)
    else:
        for r in range(own_rows):
            rows[:, r, :] = pv[:, r * extent : (r + 1) * extent]
    tables(other, False)

    pl.semaphore_wait(barrier, half + 1)
    by_role(far_leg_copy)

    @pl.loop(0, half)
    def _(s):
        def store(m, value):
            lnear[s, m] = value

        pick_legs(s, rows, store)

    @pl.loop(1, half)
    def _(t):
        near_leg_copy(t).start()

    x_copy.wait()

    @pl.loop(0, half)
    def _(s):
        for j in range(own_a):
            xnear[s, j] = xs[ids_ref[base + s], j]

    def start_near(c):
        @pl.loop(1, half)
        def _(t):
            near_copy(c, t).start()

    start_near(0)
    pl.when(jnp.logical_not(is_gate))(lambda: start_near(1))

    @pl.loop(0, slots)
    def _(k):
        source = lax.fori_loop(
            0,
            half,
            lambda s, v: v + jnp.where(first_ref[s] == k, ids_ref[other + s], 0),
            jnp.int32(0),
            unroll=True,
        )
        for j in range(own_a):
            xfar[j, k] = xs[source, j]

    for j in range(own_a):
        by_role(functools.partial(far_copy, j=j))

    @pl.when(is_gate)
    def _():
        for part, kind in enumerate(kinds):
            far_leg_copy(kind).wait_recv()

            @pl.loop(0, half)
            def _(s):
                def store(m, value):
                    lfwd[part, s, m] = value

                pick_legs(s, leg_gate[kind], store)

            lbuf[owner[kind] + lane] = lfwd[part, own]

            @pl.loop(1, half)
            def _(t):
                pass_leg_copy(kind, t).start()

        start_near(1)

    tables(base, True)

    @pl.loop(0, extent)
    def _(b):
        acc[pl.ds(pl.multiple_of(b * extent, extent), extent), :] = jnp.zeros(
            (extent, extent), jnp.float32
        )

    lbuf[me] = lnear[own]
    for c in range(2):
        for j in range(near):
            xall[(c * half + own) * near + j] = xnear[own, c * near + j]

    factors = []
    for d in range(MOST):
        value = weights_ref[jnp.minimum(start_ref[me] + d, diagrams - 1)]
        factors.append(jnp.where(d < counts_ref[me], value, 0.0))

    take(lbuf.at[pl.ds(0, half - 1)], lrecv.at[0])
    take_lanes(lambda lanes: lbuf.at[pl.ds(0, 2 * lanes)], grecv.at[0])

    @pl.loop(0, MOST * LEGS)
    def _(m):
        for v in range(workers):
            low = pl.multiple_of(m * extent, extent) + v * own_rows
            legs[pl.ds(low, own_rows), :] = lbuf[v, m].astype(jnp.float32)

    def leg(m):
        return legs[m * extent : (m + 1) * extent, :]

    firsts = []
    for d in range(MOST):
        firsts.append(leg(LEGS * d).astype(jnp.bfloat16))
        p2s[d * extent : (d + 1) * extent, :] = leg(LEGS * d + 1).astype(jnp.bfloat16)
        p3s[d] = leg(LEGS * d + 2).T.astype(jnp.bfloat16)
    wall = jnp.concatenate(firsts, axis=1)
    width = MOST * size
    at = lax.broadcasted_iota(jnp.int32, (MOST * extent, width), 0)
    for g in range(groups):
        chosen = jnp.where(at == key_ref[side, g], 1.0, 0.0).astype(jnp.bfloat16)
        p1s[g] = jnp.dot(wall, chosen, preferred_element_type=jnp.float32).astype(jnp.bfloat16)

    def forward(kind, j):
        part = kinds.index(kind)

        @pl.when(is_gate)
        def _():
            far_copy(kind, j).wait_recv()

            @pl.loop(0, half)
            def _(s):
                fwd[part, j, s] = gate[kind][j][slot_ref[s]]

            xall[low_of[kind] + j * quarter + lane] = fwd[part, j, own]

            @pl.loop(1, half)
            def _(t):
                pass_copy(kind, j, t).start()

    near_steps, item_steps = size // GROUP, quarter // GROUP
    begin = 2 * near_steps
    main_steps = begin + item_steps * main
    last_steps = item_steps * (len(items) - main)
    last = last_steps * GROUP
    rank = 2 * WIDE + PAD

    def reached(value, limit):
        span = 2 * workers * own_a
        return lax.div(value - limit + span, span)

    def pieces(b, columns, count):
        cols = [
            mid[pl.ds(WIDE * b + h, MOST * count, stride=step), :].astype(jnp.bfloat16)
            for h in range(WIDE)
        ]
        t = jnp.dot(columns, jnp.concatenate(cols, axis=1), preferred_element_type=jnp.float32)
        out = []
        for h in range(WIDE):
            at = pl.ds(pl.multiple_of((WIDE * b + h) * extent, 8), extent)
            out.append((at, t[:, h * extent : (h + 1) * extent] + acc[at, :]))
        return out

    @pl.loop(0, main_steps + last_steps)
    def _(st):
        for f, (kind, j) in enumerate(items):
            pl.when(st == when[f])(functools.partial(forward, kind, j))

        for c in range(2):

            @pl.when(st == c * near_steps)
            def _():
                take(xall.at[pl.ds(0, (half - 1) * near)], nrecv.at[c])

        past = reached(st, begin)
        i = lax.div(past * (st - begin), item_steps)
        inside = lax.rem(past * (st - begin), item_steps)
        middle, end = reached(i, early), reached(i, early + own_a)
        part = 1 - middle + end
        j = i - middle * early - end * (own_a - early)
        low = half * own_a + (part * own_a + j) * quarter

        @pl.when(jnp.logical_and(past == 1, inside == 0))
        def _():
            take_lanes(lambda lanes: xall.at[pl.ds(0, lanes)], frecv.at[part, j])

        x_at = (1 - past) * st * GROUP + past * (low + inside * GROUP)
        final = reached(st, main_steps)
        stride = size + final * (last - size)
        start = ((1 - final) * lax.rem(st, near_steps) + final * (st - main_steps)) * GROUP
        both = jnp.concatenate([xall[x_at + n] for n in range(GROUP)], axis=1)
        for d in range(MOST):
            z = jnp.dot(
                p2s[d * extent : (d + 1) * extent, :], both, preferred_element_type=jnp.float32
            ).astype(jnp.bfloat16)
            stacked = jnp.concatenate(
                [z[:, n * extent : (n + 1) * extent] for n in range(GROUP)], axis=0
            )
            y = jnp.dot(stacked, p3s[d], preferred_element_type=jnp.float32) * factors[d]
            for n in range(GROUP):
                at = pl.multiple_of((d * stride + start + n) * step, 8)
                mid[pl.ds(at, extent), :] = y[n * extent : (n + 1) * extent]

        full = jnp.logical_and(st < main_steps, lax.rem(st, near_steps) == near_steps - 1)

        @pl.when(jnp.logical_or(full, st == main_steps - 1))
        def _():
            g = lax.div(st, near_steps)

            @pl.loop(0, extent // WIDE)
            def _(b):
                for at, piece in pieces(b, p1s[g], size):
                    acc[at, :] = piece

    @pl.loop(0, extent // (2 * WIDE))
    def _(b):
        for part in range(2):
            for h, (at, piece) in enumerate(
                pieces(2 * b + part, p1s[groups - 1, :, : MOST * last], last)
            ):
                stage[pl.ds(part * WIDE + h, extent, stride=rank), :] = piece
        at = pl.ds(pl.multiple_of(2 * WIDE * b, 2 * WIDE), 2 * WIDE)
        done = stage[...].reshape(extent, rank, extent)[:, : 2 * WIDE, :]
        o_ref[:, at, :] = done.astype(jnp.bfloat16)

    take(lnear.at[pl.ds(0, half - 1)], lsend.at[0])
    far_leg_copy("far").wait_send()
    take(xnear.at[pl.ds(0, half - 1)], nsend.at[0])
    take(xfar, csend.at[0])

    @pl.when(is_gate)
    def _():
        take(lfwd.at[:, pl.ds(0, half - 1)], gsend.at[0])
        take(fwd.at[:, :, pl.ds(0, half - 1)], fsend.at[0])


def contract(x, perambs, ids, pids, counts, weights, *, workers, slots, number):
    own_a, extent = x.shape[1], x.shape[2]
    own_rows = own_a
    half, quarter = workers // 2, workers // 4
    _, _, size, groups, _, _, keys = plan(workers, own_a, slots)
    step = extent + PAD
    smem = pl.BlockSpec(memory_space=pltpu.SMEM)
    hbm = pl.BlockSpec(memory_space=pltpu.HBM)
    slab = (extent, extent)
    bf16, f32 = jnp.bfloat16, jnp.float32
    legs = MOST * LEGS
    pieces = (perambs.shape[0], own_rows, extent)
    dma = pltpu.SemaphoreType.DMA
    return pl.pallas_call(
        functools.partial(contract_kernel, workers, slots),
        out_shape=jax.ShapeDtypeStruct((extent, extent, extent), bf16),
        in_specs=[smem, smem, smem, smem, pl.BlockSpec(memory_space=pltpu.VMEM), hbm, hbm],
        out_specs=pl.BlockSpec(memory_space=pltpu.VMEM),
        scratch_shapes=[
            pltpu.VMEM(x.shape, bf16),
            pltpu.VMEM(perambs.shape, bf16),
            pltpu.VMEM(pieces, bf16),
            pltpu.VMEM((half, own_a) + slab, bf16),
            pltpu.VMEM((own_a, slots) + slab, bf16),
            pltpu.VMEM((half, legs, own_rows, extent), bf16),
            pltpu.VMEM(pieces, bf16),
            pltpu.VMEM(pieces, bf16),
            pltpu.VMEM((2, half, legs, own_rows, extent), bf16),
            pltpu.VMEM((workers * own_a,) + slab, bf16),
            pltpu.VMEM((workers, legs, own_rows, extent), bf16),
            pltpu.VMEM((2, own_a, half) + slab, bf16),
            pltpu.VMEM((legs * extent, extent), f32),
            pltpu.VMEM((groups, extent, MOST * size), bf16),
            pltpu.VMEM((MOST * extent, extent), bf16),
            pltpu.VMEM((MOST,) + slab, bf16),
            pltpu.VMEM((MOST * size * step, extent), f32),
            pltpu.VMEM((extent * extent, extent), f32),
            pltpu.VMEM((extent * (2 * WIDE + PAD), extent), f32),
            pltpu.SMEM((half,), jnp.int32),
            pltpu.SMEM((half,), jnp.int32),
            pltpu.SMEM((half,), jnp.int32),
            pltpu.SMEM((workers,), jnp.int32),
            dma((2,)),
            dma((1,)),
            dma((1,)),
            dma((1,)),
            dma((2,)),
            dma((1,)),
            dma((1,)),
            dma((1,)),
            dma((2,)),
            dma((1,)),
            dma((2, own_a)),
            dma((1,)),
            dma((2, own_a)),
        ]
        + [pltpu.VMEM((slots,) + slab, bf16) for _ in range(2 * own_a)],
        compiler_params=pltpu.CompilerParams(
            vmem_limit_bytes=48 * 1024 * 1024, collective_id=number, has_side_effects=True
        ),
        name=f"contract_{slots}",
    )(ids, pids, counts, weights, jnp.asarray(keys, jnp.int32), x, perambs)


def choose_kernel(caps, ids_ref, o_ref):
    half = ids_ref.shape[0] // 2

    def distinct(low):
        def one(s, count):
            v = ids_ref[low + s]
            seen = lax.fori_loop(
                0,
                half,
                lambda k, m: m + jnp.where(jnp.logical_and(k < s, ids_ref[low + k] == v), 1, 0),
                jnp.int32(0),
                unroll=True,
            )
            return count + jnp.where(seen == 0, 1, 0)

        return lax.fori_loop(0, half, one, jnp.int32(0), unroll=half <= 8)

    most = jnp.maximum(distinct(0), distinct(half))
    which = jnp.int32(0)
    for cap in caps[:-1]:
        which = which + jnp.where(most > cap, 1, 0)
    o_ref[0] = which


def choose(ids, caps):
    smem = pl.BlockSpec(memory_space=pltpu.SMEM)
    return pl.pallas_call(
        functools.partial(choose_kernel, caps),
        out_shape=jax.ShapeDtypeStruct((1,), jnp.int32),
        in_specs=[smem],
        out_specs=smem,
        name="choose",
    )(ids)[0]


def per_device(sources, perambs, source_ids, peramb_ids, sink_counts, weights):
    workers = lax.axis_size("work")
    extent = sources.shape[2]
    own_a = sources.shape[1] // extent
    x = sources.reshape(-1, own_a, extent, extent)
    half = workers // 2
    caps = sorted({-(-half * part // 8) for part in (6, 7, 8)})
    which = choose(source_ids, caps)
    total = lax.switch(
        which,
        [
            functools.partial(contract, workers=workers, slots=cap, number=i)
            for i, cap in enumerate(caps)
        ],
        x,
        perambs,
        source_ids,
        peramb_ids.T,
        sink_counts,
        weights,
    )
    return total.reshape(1, extent * extent, extent)


def solution(mesh):
    return jax.shard_map(
        per_device,
        mesh=mesh,
        in_specs=(P("cfg", "work", None), P("cfg", "work"), P(), P(), P(), P()),
        out_specs=P(("cfg", "work"), None, None),
        check_vma=False,
    )
```

```python
import functools

import jax
import jax.numpy as jnp
import numpy as np
from jax import lax
from jax.experimental import pallas as pl
from jax.experimental.pallas import tpu as pltpu
from jax.sharding import PartitionSpec as P

MOST = 6
LEGS = 3
PAD = 8
GROUP = 4
WIDE = 8
MESH = pl.DeviceIdType.MESH


def plan(workers, own_a, slots):
    half, quarter = workers // 2, workers // 4
    near = own_a // 2
    size = half * near
    early = max(0, min(own_a - 2, int(quarter * own_a / slots - 0.33)))
    items = [("late", j) for j in range(early)]
    items += [("far", j) for j in range(own_a)]
    items += [("late", j) for j in range(early, own_a)]
    tail = max(1, 8 // quarter)
    body = len(items) - tail

    slabs = []
    for c in range(2):
        slabs += [(("near", v), c * near + j) for v in range(half) for j in range(near)]
    for kind, j in items:
        slabs += [((kind, v), j) for v in range(quarter)]
    split = 2 * size + body * quarter
    groups = [slabs[low : min(low + size, split)] for low in range(0, split, size)]
    groups.append(slabs[split:])
    keys = np.full((2, len(groups), 1, MOST * size), -1)
    for side in range(2):
        first = {
            "near": side * half,
            "far": (1 - side) * half + (1 - side) * quarter,
            "late": (1 - side) * half + side * quarter,
        }
        for g, group in enumerate(groups):
            stride = size if g < len(groups) - 1 else len(group)
            for at, ((kind, v), j) in enumerate(group):
                for d in range(MOST):
                    a = (first[kind] + v) * own_a + j
                    keys[side, g, 0, d * stride + at] = d * (workers * own_a) + a

    unit = GROUP
    near_steps, item_steps = size // unit, quarter // unit
    begin = 2 * near_steps
    when = []
    for f in range(len(items)):
        if f < 3:
            at = (0, near_steps - 1, near_steps)[f]
        elif f == 3 and early > 3:
            at = begin - 1
        elif f < body:
            at = begin + item_steps * (f - 2)
        elif f < len(items) - 1:
            at = begin + item_steps * (f - 1)
        else:
            at = begin + item_steps * body
        when.append(min(at, begin + item_steps * f))
    return items, early, size, len(groups), body, when, keys


def contract_kernel(
    workers,
    slots,
    ids_ref,
    pids_ref,
    counts_ref,
    weights_ref,
    key_ref,
    x_hbm,
    p_hbm,
    o_ref,
    xs,
    pv,
    rows,
    xnear,
    xfar,
    xlast,
    lnear,
    lgate,
    lgate_late,
    lfwd,
    xall,
    lbuf,
    fwd,
    legs,
    p1s,
    p2s,
    p3s,
    mid,
    acc,
    stage,
    first_ref,
    rank_ref,
    slot_ref,
    start_ref,
    in_sem,
    lsend,
    lrecv,
    msend,
    mrecv,
    gsend,
    grecv,
    nsend,
    nrecv,
    csend,
    dsend,
    crecv,
    fsend,
    frecv,
    *gates,
):
    own_a, extent = xs.shape[1], xs.shape[3]
    own_rows = lbuf.shape[2]
    diagrams = weights_ref.shape[0]
    half, quarter = workers // 2, workers // 4
    near = own_a // 2
    items, early, size, groups, main, when, _ = plan(workers, own_a, slots)
    kinds = ("far", "late")
    gate = {"far": gates[:own_a], "late": gates[own_a:]}
    leg_gate = {"far": lgate, "late": lgate_late}
    low_of = {"far": half * own_a, "late": (half + quarter) * own_a}
    step = extent + PAD
    me = lax.axis_index("work")
    side = lax.div(me, half)
    own = lax.rem(me, half)
    lane = lax.rem(me, quarter)
    sub = lax.div(own, quarter)
    base = side * half
    other = (1 - side) * half
    is_gate = sub == 1 - side
    far_gate = lane + quarter * (2 - side)
    owner = {"far": other + (1 - side) * quarter, "late": other + side * quarter}

    p_copy = pltpu.make_async_copy(p_hbm, pv, in_sem.at[0])
    x_copy = pltpu.make_async_copy(x_hbm, xs, in_sem.at[1])
    p_copy.start()
    x_copy.start()

    barrier = pltpu.get_barrier_semaphore()

    def greet(peer):
        pl.semaphore_signal(barrier, inc=1, device_id={"work": peer}, device_id_type=MESH)

    @pl.loop(1, half)
    def _(t):
        greet(base + lax.rem(own + t, half))

    @pl.loop(0, quarter)
    def _(via):
        greet(other + side * quarter + via)

    @pl.when(is_gate)
    def _():
        greet(other + (1 - side) * quarter + lane)

    def tables(low, with_slots):
        def ranked(s, count):
            v = ids_ref[low + s]
            first = lax.fori_loop(
                0,
                half,
                lambda k, m: jnp.minimum(m, jnp.where(ids_ref[low + k] == v, k, half)),
                jnp.int32(half),
                unroll=True,
            )
            is_first = first == s
            first_ref[s] = jnp.where(is_first, count, -1)
            rank_ref[s] = count
            if with_slots:
                slot_ref[s] = rank_ref[first]
            return count + jnp.where(is_first, 1, 0)

        lax.fori_loop(0, half, ranked, jnp.int32(0))

    def start_of(s, start):
        start_ref[s] = start
        return start + counts_ref[s]

    lax.fori_loop(0, workers, start_of, jnp.int32(0))

    def pick_legs(s, source, store):
        for slot in range(MOST):
            d = jnp.minimum(start_ref[base + s] + slot, diagrams - 1)
            for leg in range(LEGS):
                store(slot * LEGS + leg, source[pids_ref[leg, d]])

    def near_leg_copy(t):
        to = lax.rem(own + t, half)
        return pltpu.make_async_remote_copy(
            src_ref=lnear.at[to],
            dst_ref=lbuf.at[me],
            send_sem=lsend.at[0],
            recv_sem=lrecv.at[0],
            device_id={"work": base + to},
            device_id_type=MESH,
        )

    def far_leg_copy(kind):
        return pltpu.make_async_remote_copy(
            src_ref=rows,
            dst_ref=leg_gate[kind],
            send_sem=msend.at[0],
            recv_sem=mrecv.at[kinds.index(kind)],
            device_id={"work": far_gate},
            device_id_type=MESH,
        )

    def pass_leg_copy(kind, t):
        part = kinds.index(kind)
        to = lax.rem(own + t, half)
        return pltpu.make_async_remote_copy(
            src_ref=lfwd.at[part, to],
            dst_ref=lbuf.at[owner[kind] + lane],
            send_sem=gsend.at[0],
            recv_sem=grecv.at[0],
            device_id={"work": base + to},
            device_id_type=MESH,
        )

    def take(ref, sem):
        pltpu.make_async_copy(ref, ref, sem).wait()

    def take_lanes(ref_of, sem):
        pl.when(is_gate)(lambda: take(ref_of(quarter - 1), sem))
        pl.when(jnp.logical_not(is_gate))(lambda: take(ref_of(quarter), sem))

    def near_copy(c, t):
        to = lax.rem(own + t, half)
        return pltpu.make_async_remote_copy(
            src_ref=xnear.at[to, pl.ds(c * near, near)],
            dst_ref=xall.at[pl.ds((c * half + own) * near, near)],
            send_sem=nsend.at[0],
            recv_sem=nrecv.at[c],
            device_id={"work": base + to},
            device_id_type=MESH,
        )

    def far_copy(kind, j):
        return pltpu.make_async_remote_copy(
            src_ref=xfar.at[j],
            dst_ref=gate[kind][j],
            send_sem=csend.at[0],
            recv_sem=crecv.at[kinds.index(kind), j],
            device_id={"work": far_gate},
            device_id_type=MESH,
        )

    def pass_copy(kind, j, t):
        part = kinds.index(kind)
        to = lax.rem(own + t, half)
        return pltpu.make_async_remote_copy(
            src_ref=fwd.at[part, j, to],
            dst_ref=xall.at[low_of[kind] + j * quarter + lane],
            send_sem=fsend.at[part],
            recv_sem=frecv.at[part, j],
            device_id={"work": base + to},
            device_id_type=MESH,
        )

    def last_copy(to):
        return pltpu.make_async_remote_copy(
            src_ref=xlast.at[to],
            dst_ref=xall.at[low_of["late"] + (own_a - 1) * quarter + lane],
            send_sem=dsend.at[0],
            recv_sem=frecv.at[1, own_a - 1],
            device_id={"work": other + to},
            device_id_type=MESH,
        )

    def by_role(make):
        pl.when(is_gate)(make("late").start)
        pl.when(jnp.logical_not(is_gate))(make("far").start)

    p_copy.wait()
    total = rows.shape[0]
    if own_rows % 8 == 0 and total * own_rows <= legs.shape[0]:
        for r in range(own_rows):
            piece = pv[:, r * extent : (r + 1) * extent].astype(jnp.float32)
            legs[pl.ds(r, total, stride=own_rows), :] = piece
        whole = legs[: total * own_rows, :].reshape(total, own_rows, extent)
        rows[...] = whole.astype(jnp.bfloat16)
    else:
        for r in range(own_rows):
            rows[:, r, :] = pv[:, r * extent : (r + 1) * extent]
    tables(other, False)

    pl.when(is_gate)(lambda: pl.semaphore_wait(barrier, 2 * half - 1))
    pl.when(jnp.logical_not(is_gate))(lambda: pl.semaphore_wait(barrier, half))
    by_role(far_leg_copy)

    @pl.loop(0, half)
    def _(s):
        def store(m, value):
            lnear[s, m] = value

        pick_legs(s, rows, store)

    @pl.loop(1, half)
    def _(t):
        near_leg_copy(t).start()

    x_copy.wait()

    @pl.loop(0, half)
    def _(s):
        for j in range(own_a):
            xnear[s, j] = xs[ids_ref[base + s], j]

    def start_near(c):
        @pl.loop(1, half)
        def _(t):
            near_copy(c, t).start()

    start_near(0)
    pl.when(jnp.logical_not(is_gate))(lambda: start_near(1))

    @pl.loop(0, slots)
    def _(k):
        source = lax.fori_loop(
            0,
            half,
            lambda s, v: v + jnp.where(first_ref[s] == k, ids_ref[other + s], 0),
            jnp.int32(0),
            unroll=True,
        )
        for j in range(own_a):
            xfar[j, k] = xs[source, j]

    @pl.loop(0, half)
    def _(s):
        xlast[s] = xs[ids_ref[other + s], own_a - 1]

    for j in range(own_a - 1):
        by_role(functools.partial(far_copy, j=j))
    pl.when(jnp.logical_not(is_gate))(far_copy("far", own_a - 1).start)

    @pl.when(is_gate)
    def _():
        @pl.loop(0, half)
        def _(n):
            last_copy(lax.rem(n + side * quarter, half)).start()

    @pl.when(is_gate)
    def _():
        for part, kind in enumerate(kinds):
            far_leg_copy(kind).wait_recv()

            @pl.loop(0, half)
            def _(s):
                def store(m, value):
                    lfwd[part, s, m] = value

                pick_legs(s, leg_gate[kind], store)

            lbuf[owner[kind] + lane] = lfwd[part, own]

            @pl.loop(1, half)
            def _(t):
                pass_leg_copy(kind, t).start()

        start_near(1)

    tables(base, True)

    @pl.loop(0, extent)
    def _(b):
        acc[pl.ds(pl.multiple_of(b * extent, extent), extent), :] = jnp.zeros(
            (extent, extent), jnp.float32
        )

    lbuf[me] = lnear[own]
    for c in range(2):
        for j in range(near):
            xall[(c * half + own) * near + j] = xnear[own, c * near + j]

    factors = []
    for d in range(MOST):
        value = weights_ref[jnp.minimum(start_ref[me] + d, diagrams - 1)]
        factors.append(jnp.where(d < counts_ref[me], value, 0.0))

    take(lbuf.at[pl.ds(0, half - 1)], lrecv.at[0])
    take_lanes(lambda lanes: lbuf.at[pl.ds(0, 2 * lanes)], grecv.at[0])

    @pl.loop(0, MOST * LEGS)
    def _(m):
        for v in range(workers):
            low = pl.multiple_of(m * extent, extent) + v * own_rows
            legs[pl.ds(low, own_rows), :] = lbuf[v, m].astype(jnp.float32)

    def leg(m):
        return legs[m * extent : (m + 1) * extent, :]

    firsts = []
    for d in range(MOST):
        firsts.append(leg(LEGS * d).astype(jnp.bfloat16))
        p2s[d * extent : (d + 1) * extent, :] = leg(LEGS * d + 1).astype(jnp.bfloat16)
        p3s[d] = leg(LEGS * d + 2).T.astype(jnp.bfloat16)
    wall = jnp.concatenate(firsts, axis=1)
    width = MOST * size
    at = lax.broadcasted_iota(jnp.int32, (MOST * extent, width), 0)
    for g in range(groups):
        chosen = jnp.where(at == key_ref[side, g], 1.0, 0.0).astype(jnp.bfloat16)
        p1s[g] = jnp.dot(wall, chosen, preferred_element_type=jnp.float32).astype(jnp.bfloat16)

    def forward(kind, j):
        part = kinds.index(kind)

        @pl.when(is_gate)
        def _():
            far_copy(kind, j).wait_recv()

            @pl.loop(0, half)
            def _(s):
                fwd[part, j, s] = gate[kind][j][slot_ref[s]]

            xall[low_of[kind] + j * quarter + lane] = fwd[part, j, own]

            @pl.loop(1, half)
            def _(t):
                pass_copy(kind, j, t).start()

    near_steps, item_steps = size // GROUP, quarter // GROUP
    begin = 2 * near_steps
    main_steps = begin + item_steps * main
    last_steps = item_steps * (len(items) - main)
    last = last_steps * GROUP
    rank = 2 * WIDE + PAD

    def reached(value, limit):
        span = 2 * workers * own_a
        return lax.div(value - limit + span, span)

    def pieces(b, columns, count):
        cols = [
            mid[pl.ds(WIDE * b + h, MOST * count, stride=step), :].astype(jnp.bfloat16)
            for h in range(WIDE)
        ]
        t = jnp.dot(columns, jnp.concatenate(cols, axis=1), preferred_element_type=jnp.float32)
        out = []
        for h in range(WIDE):
            at = pl.ds(pl.multiple_of((WIDE * b + h) * extent, 8), extent)
            out.append((at, t[:, h * extent : (h + 1) * extent] + acc[at, :]))
        return out

    @pl.loop(0, main_steps + last_steps)
    def _(st):
        for f, (kind, j) in enumerate(items[:-1]):
            pl.when(st == when[f])(functools.partial(forward, kind, j))

        for c in range(2):

            @pl.when(st == c * near_steps)
            def _():
                take(xall.at[pl.ds(0, (half - 1) * near)], nrecv.at[c])

        past = reached(st, begin)
        i = lax.div(past * (st - begin), item_steps)
        inside = lax.rem(past * (st - begin), item_steps)
        middle, end = reached(i, early), reached(i, early + own_a)
        part = 1 - middle + end
        j = i - middle * early - end * (own_a - early)
        low = half * own_a + (part * own_a + j) * quarter

        @pl.when(jnp.logical_and(past == 1, inside == 0))
        def _():
            direct = i == len(items) - 1

            @pl.when(direct)
            def _():
                take(xall.at[pl.ds(0, quarter)], frecv.at[part, j])

            @pl.when(jnp.logical_not(direct))
            def _():
                take_lanes(lambda lanes: xall.at[pl.ds(0, lanes)], frecv.at[part, j])

        x_at = (1 - past) * st * GROUP + past * (low + inside * GROUP)
        final = reached(st, main_steps)
        stride = size + final * (last - size)
        start = ((1 - final) * lax.rem(st, near_steps) + final * (st - main_steps)) * GROUP
        both = jnp.concatenate([xall[x_at + n] for n in range(GROUP)], axis=1)
        for d in range(MOST):
            z = jnp.dot(
                p2s[d * extent : (d + 1) * extent, :], both, preferred_element_type=jnp.float32
            ).astype(jnp.bfloat16)
            stacked = jnp.concatenate(
                [z[:, n * extent : (n + 1) * extent] for n in range(GROUP)], axis=0
            )
            y = jnp.dot(stacked, p3s[d], preferred_element_type=jnp.float32) * factors[d]
            for n in range(GROUP):
                at = pl.multiple_of((d * stride + start + n) * step, 8)
                mid[pl.ds(at, extent), :] = y[n * extent : (n + 1) * extent]

        full = jnp.logical_and(st < main_steps, lax.rem(st, near_steps) == near_steps - 1)

        @pl.when(jnp.logical_or(full, st == main_steps - 1))
        def _():
            g = lax.div(st, near_steps)

            @pl.loop(0, extent // WIDE)
            def _(b):
                for at, piece in pieces(b, p1s[g], size):
                    acc[at, :] = piece

    @pl.loop(0, extent // (2 * WIDE))
    def _(b):
        for part in range(2):
            for h, (at, piece) in enumerate(
                pieces(2 * b + part, p1s[groups - 1, :, : MOST * last], last)
            ):
                stage[pl.ds(part * WIDE + h, extent, stride=rank), :] = piece
        at = pl.ds(pl.multiple_of(2 * WIDE * b, 2 * WIDE), 2 * WIDE)
        done = stage[...].reshape(extent, rank, extent)[:, : 2 * WIDE, :]
        o_ref[:, at, :] = done.astype(jnp.bfloat16)

    take(lnear.at[pl.ds(0, half - 1)], lsend.at[0])
    far_leg_copy("far").wait_send()
    take(xnear.at[pl.ds(0, half - 1)], nsend.at[0])
    pl.when(jnp.logical_not(is_gate))(lambda: take(xfar, csend.at[0]))

    @pl.when(is_gate)
    def _():
        take(lfwd.at[:, pl.ds(0, half - 1)], gsend.at[0])
        take(fwd.at[0, :, pl.ds(0, half - 1)], fsend.at[0])
        take(fwd.at[1, pl.ds(0, own_a - 1), pl.ds(0, half - 1)], fsend.at[1])
        take(xfar.at[pl.ds(0, own_a - 1)], csend.at[0])
        take(xlast, dsend.at[0])


def contract(x, perambs, ids, pids, counts, weights, *, workers, slots, number):
    own_a, extent = x.shape[1], x.shape[2]
    own_rows = own_a
    half, quarter = workers // 2, workers // 4
    _, _, size, groups, _, _, keys = plan(workers, own_a, slots)
    step = extent + PAD
    smem = pl.BlockSpec(memory_space=pltpu.SMEM)
    hbm = pl.BlockSpec(memory_space=pltpu.HBM)
    slab = (extent, extent)
    bf16, f32 = jnp.bfloat16, jnp.float32
    legs = MOST * LEGS
    pieces = (perambs.shape[0], own_rows, extent)
    dma = pltpu.SemaphoreType.DMA
    return pl.pallas_call(
        functools.partial(contract_kernel, workers, slots),
        out_shape=jax.ShapeDtypeStruct((extent, extent, extent), bf16),
        in_specs=[smem, smem, smem, smem, pl.BlockSpec(memory_space=pltpu.VMEM), hbm, hbm],
        out_specs=pl.BlockSpec(memory_space=pltpu.VMEM),
        scratch_shapes=[
            pltpu.VMEM(x.shape, bf16),
            pltpu.VMEM(perambs.shape, bf16),
            pltpu.VMEM(pieces, bf16),
            pltpu.VMEM((half, own_a) + slab, bf16),
            pltpu.VMEM((own_a, slots) + slab, bf16),
            pltpu.VMEM((half,) + slab, bf16),
            pltpu.VMEM((half, legs, own_rows, extent), bf16),
            pltpu.VMEM(pieces, bf16),
            pltpu.VMEM(pieces, bf16),
            pltpu.VMEM((2, half, legs, own_rows, extent), bf16),
            pltpu.VMEM((workers * own_a,) + slab, bf16),
            pltpu.VMEM((workers, legs, own_rows, extent), bf16),
            pltpu.VMEM((2, own_a, half) + slab, bf16),
            pltpu.VMEM((legs * extent, extent), f32),
            pltpu.VMEM((groups, extent, MOST * size), bf16),
            pltpu.VMEM((MOST * extent, extent), bf16),
            pltpu.VMEM((MOST,) + slab, bf16),
            pltpu.VMEM((MOST * size * step, extent), f32),
            pltpu.VMEM((extent * extent, extent), f32),
            pltpu.VMEM((extent * (2 * WIDE + PAD), extent), f32),
            pltpu.SMEM((half,), jnp.int32),
            pltpu.SMEM((half,), jnp.int32),
            pltpu.SMEM((half,), jnp.int32),
            pltpu.SMEM((workers,), jnp.int32),
            dma((2,)),
            dma((1,)),
            dma((1,)),
            dma((1,)),
            dma((2,)),
            dma((1,)),
            dma((1,)),
            dma((1,)),
            dma((2,)),
            dma((1,)),
            dma((1,)),
            dma((2, own_a)),
            dma((2,)),
            dma((2, own_a)),
        ]
        + [pltpu.VMEM((slots,) + slab, bf16) for _ in range(2 * own_a - 1)],
        compiler_params=pltpu.CompilerParams(
            vmem_limit_bytes=48 * 1024 * 1024, collective_id=number, has_side_effects=True
        ),
        name=f"contract_{slots}",
    )(ids, pids, counts, weights, jnp.asarray(keys, jnp.int32), x, perambs)


def choose_kernel(caps, ids_ref, o_ref):
    half = ids_ref.shape[0] // 2

    def distinct(low):
        def one(s, count):
            v = ids_ref[low + s]
            seen = lax.fori_loop(
                0,
                half,
                lambda k, m: m + jnp.where(jnp.logical_and(k < s, ids_ref[low + k] == v), 1, 0),
                jnp.int32(0),
                unroll=True,
            )
            return count + jnp.where(seen == 0, 1, 0)

        return lax.fori_loop(0, half, one, jnp.int32(0), unroll=half <= 8)

    most = jnp.maximum(distinct(0), distinct(half))
    which = jnp.int32(0)
    for cap in caps[:-1]:
        which = which + jnp.where(most > cap, 1, 0)
    o_ref[0] = which


def choose(ids, caps):
    smem = pl.BlockSpec(memory_space=pltpu.SMEM)
    return pl.pallas_call(
        functools.partial(choose_kernel, caps),
        out_shape=jax.ShapeDtypeStruct((1,), jnp.int32),
        in_specs=[smem],
        out_specs=smem,
        name="choose",
    )(ids)[0]


def per_device(sources, perambs, source_ids, peramb_ids, sink_counts, weights):
    workers = lax.axis_size("work")
    extent = sources.shape[2]
    own_a = sources.shape[1] // extent
    x = sources.reshape(-1, own_a, extent, extent)
    half = workers // 2
    caps = sorted({-(-half * part // 8) for part in (6, 7, 8)})
    which = choose(source_ids, caps)
    total = lax.switch(
        which,
        [
            functools.partial(contract, workers=workers, slots=cap, number=i)
            for i, cap in enumerate(caps)
        ],
        x,
        perambs,
        source_ids,
        peramb_ids.T,
        sink_counts,
        weights,
    )
    return total.reshape(1, extent * extent, extent)


def solution(mesh):
    return jax.shard_map(
        per_device,
        mesh=mesh,
        in_specs=(P("cfg", "work", None), P("cfg", "work"), P(), P(), P(), P()),
        out_specs=P(("cfg", "work"), None, None),
        check_vma=False,
    )
```

```python
import functools

import jax
import jax.numpy as jnp
import numpy as np
from jax import lax
from jax.experimental import pallas as pl
from jax.experimental.pallas import tpu as pltpu
from jax.sharding import PartitionSpec as P

MOST = 6
LEGS = 3
PAD = 8
GROUP = 4
WIDE = 8
MESH = pl.DeviceIdType.MESH


def plan(workers, own_a, slots):
    half, quarter = workers // 2, workers // 4
    near = own_a // 2
    size = half * near
    early = max(0, min(own_a - 2, int(1.5 * quarter * own_a / slots - 2.9)))
    items = [("late", j) for j in range(early)]
    items += [("far", j) for j in range(own_a)]
    items += [("late", j) for j in range(early, own_a)]
    tail = max(1, 8 // quarter)
    body = len(items) - tail

    groups = 3 - (-body * quarter // size)

    unit = GROUP
    near_steps, item_steps = size // unit, quarter // unit
    begin = 2 * near_steps
    when = []
    for f in range(len(items)):
        if f < 3:
            at = (0, near_steps - 1, near_steps)[f]
        elif f == 3 and early > 3:
            at = begin - 1
        elif f < body:
            at = begin + item_steps * (f - 2)
        elif f < len(items) - 1:
            at = begin + item_steps * (f - 1)
        else:
            at = begin + item_steps * body
        when.append(min(at, begin + item_steps * f))
    return items, early, size, groups, body, when


def log2(n):
    assert n & (n - 1) == 0
    return n.bit_length() - 1


def key_row(g, side, workers, own_a, slots):
    items, early, size, groups, body, _ = plan(workers, own_a, slots)
    half, quarter = workers // 2, workers // 4
    near = own_a // 2
    last = (len(items) - body) * quarter
    stride = size if g < groups - 1 else last
    col = lax.broadcasted_iota(jnp.int32, (1, MOST * size), 1)
    d = lax.shift_right_logical(col, jnp.int32(log2(stride)))
    pos = col & (stride - 1)
    if g < 2:
        v = side * half + lax.shift_right_logical(pos, jnp.int32(log2(near)))
        j = g * near + (pos & (near - 1))
        valid = col >= 0
    else:
        first = (g - 2) * (size // quarter) if g < groups - 1 else body
        item = first + lax.shift_right_logical(pos, jnp.int32(log2(quarter)))
        middle = jnp.where(item >= early, 1, 0)
        end = jnp.where(item >= early + own_a, 1, 0)
        part = 1 - middle + end
        j = item - middle * early - end * (own_a - early)
        sub = (1 - side) + part * (2 * side - 1)
        v = (1 - side) * half + sub * quarter + (pos & (quarter - 1))
        valid = item < body if g < groups - 1 else col < MOST * last
    return jnp.where(valid, d * (workers * own_a) + v * own_a + j, -1)


def contract_kernel(
    workers,
    slots,
    ids_ref,
    pids_ref,
    counts_ref,
    weights_ref,
    x_hbm,
    p_hbm,
    o_ref,
    xs,
    pv,
    rows,
    xnear,
    xfar,
    xlast,
    lnear,
    lgate,
    lgate_late,
    lfwd,
    xall,
    lbuf,
    fwd,
    legs,
    p1s,
    p2s,
    p3s,
    mid,
    acc,
    stage,
    first_ref,
    rank_ref,
    slot_ref,
    start_ref,
    in_sem,
    lsend,
    lrecv,
    msend,
    mrecv,
    gsend,
    grecv,
    nsend,
    nrecv,
    csend,
    dsend,
    crecv,
    fsend,
    frecv,
    *gates,
):
    own_a, extent = xs.shape[1], xs.shape[3]
    own_rows = lbuf.shape[2]
    diagrams = weights_ref.shape[0]
    half, quarter = workers // 2, workers // 4
    near = own_a // 2
    items, early, size, groups, main, when = plan(workers, own_a, slots)
    kinds = ("far", "late")
    gate = {"far": gates[:own_a], "late": gates[own_a:]}
    leg_gate = {"far": lgate, "late": lgate_late}
    low_of = {"far": half * own_a, "late": (half + quarter) * own_a}
    step = extent + PAD
    me = lax.axis_index("work")
    side = lax.div(me, half)
    own = lax.rem(me, half)
    lane = lax.rem(me, quarter)
    sub = lax.div(own, quarter)
    base = side * half
    other = (1 - side) * half
    is_gate = sub == 1 - side
    far_gate = lane + quarter * (2 - side)
    owner = {"far": other + (1 - side) * quarter, "late": other + side * quarter}

    p_copy = pltpu.make_async_copy(p_hbm, pv, in_sem.at[0])
    x_copy = pltpu.make_async_copy(x_hbm, xs, in_sem.at[1])
    p_copy.start()
    x_copy.start()

    barrier = pltpu.get_barrier_semaphore()

    def greet(peer):
        pl.semaphore_signal(barrier, inc=1, device_id={"work": peer}, device_id_type=MESH)

    @pl.loop(1, half)
    def _(t):
        greet(base + lax.rem(own + t, half))

    @pl.loop(0, quarter)
    def _(via):
        greet(other + side * quarter + via)

    @pl.when(is_gate)
    def _():
        greet(other + (1 - side) * quarter + lane)

    def tables(low, with_slots):
        def ranked(s, count):
            v = ids_ref[low + s]
            first = lax.fori_loop(
                0,
                half,
                lambda k, m: jnp.minimum(m, jnp.where(ids_ref[low + k] == v, k, half)),
                jnp.int32(half),
                unroll=True,
            )
            is_first = first == s
            first_ref[s] = jnp.where(is_first, count, -1)
            rank_ref[s] = count
            if with_slots:
                slot_ref[s] = rank_ref[first]
            return count + jnp.where(is_first, 1, 0)

        lax.fori_loop(0, half, ranked, jnp.int32(0))

    def start_of(s, start):
        start_ref[s] = start
        return start + counts_ref[s]

    lax.fori_loop(0, workers, start_of, jnp.int32(0))

    def pick_legs(s, source, store):
        for slot in range(MOST):
            d = jnp.minimum(start_ref[base + s] + slot, diagrams - 1)
            for leg in range(LEGS):
                store(slot * LEGS + leg, source[pids_ref[leg, d]])

    def near_leg_copy(t):
        to = lax.rem(own + t, half)
        return pltpu.make_async_remote_copy(
            src_ref=lnear.at[to],
            dst_ref=lbuf.at[me],
            send_sem=lsend.at[0],
            recv_sem=lrecv.at[0],
            device_id={"work": base + to},
            device_id_type=MESH,
        )

    def far_leg_copy(kind):
        return pltpu.make_async_remote_copy(
            src_ref=rows,
            dst_ref=leg_gate[kind],
            send_sem=msend.at[0],
            recv_sem=mrecv.at[kinds.index(kind)],
            device_id={"work": far_gate},
            device_id_type=MESH,
        )

    def pass_leg_copy(kind, t):
        part = kinds.index(kind)
        to = lax.rem(own + t, half)
        return pltpu.make_async_remote_copy(
            src_ref=lfwd.at[part, to],
            dst_ref=lbuf.at[owner[kind] + lane],
            send_sem=gsend.at[0],
            recv_sem=grecv.at[0],
            device_id={"work": base + to},
            device_id_type=MESH,
        )

    def take(ref, sem):
        pltpu.make_async_copy(ref, ref, sem).wait()

    def take_lanes(ref_of, sem):
        pl.when(is_gate)(lambda: take(ref_of(quarter - 1), sem))
        pl.when(jnp.logical_not(is_gate))(lambda: take(ref_of(quarter), sem))

    def near_copy(c, t):
        to = lax.rem(own + t, half)
        return pltpu.make_async_remote_copy(
            src_ref=xnear.at[to, pl.ds(c * near, near)],
            dst_ref=xall.at[pl.ds((c * half + own) * near, near)],
            send_sem=nsend.at[0],
            recv_sem=nrecv.at[c],
            device_id={"work": base + to},
            device_id_type=MESH,
        )

    def far_copy(kind, j):
        return pltpu.make_async_remote_copy(
            src_ref=xfar.at[j],
            dst_ref=gate[kind][j],
            send_sem=csend.at[0],
            recv_sem=crecv.at[kinds.index(kind), j],
            device_id={"work": far_gate},
            device_id_type=MESH,
        )

    def pass_copy(kind, j, t):
        part = kinds.index(kind)
        to = lax.rem(own + t, half)
        return pltpu.make_async_remote_copy(
            src_ref=fwd.at[part, j, to],
            dst_ref=xall.at[low_of[kind] + j * quarter + lane],
            send_sem=fsend.at[part],
            recv_sem=frecv.at[part, j],
            device_id={"work": base + to},
            device_id_type=MESH,
        )

    def last_copy(to):
        return pltpu.make_async_remote_copy(
            src_ref=xlast.at[to],
            dst_ref=xall.at[low_of["late"] + (own_a - 1) * quarter + lane],
            send_sem=dsend.at[0],
            recv_sem=frecv.at[1, own_a - 1],
            device_id={"work": other + to},
            device_id_type=MESH,
        )

    def by_role(make):
        pl.when(is_gate)(make("late").start)
        pl.when(jnp.logical_not(is_gate))(make("far").start)

    p_copy.wait()
    total = rows.shape[0]
    if own_rows % 8 == 0 and total * own_rows <= legs.shape[0]:
        for r in range(own_rows):
            piece = pv[:, r * extent : (r + 1) * extent].astype(jnp.float32)
            legs[pl.ds(r, total, stride=own_rows), :] = piece
        whole = legs[: total * own_rows, :].reshape(total, own_rows, extent)
        rows[...] = whole.astype(jnp.bfloat16)
    else:
        for r in range(own_rows):
            rows[:, r, :] = pv[:, r * extent : (r + 1) * extent]
    tables(other, False)

    pl.when(is_gate)(lambda: pl.semaphore_wait(barrier, 2 * half - 1))
    pl.when(jnp.logical_not(is_gate))(lambda: pl.semaphore_wait(barrier, half))
    by_role(far_leg_copy)

    @pl.loop(0, half)
    def _(s):
        def store(m, value):
            lnear[s, m] = value

        pick_legs(s, rows, store)

    @pl.loop(1, half)
    def _(t):
        near_leg_copy(t).start()

    x_copy.wait()

    @pl.loop(0, half)
    def _(s):
        for j in range(own_a):
            xnear[s, j] = xs[ids_ref[base + s], j]

    def start_near(c):
        @pl.loop(1, half)
        def _(t):
            near_copy(c, t).start()

    start_near(0)
    pl.when(jnp.logical_not(is_gate))(lambda: start_near(1))

    @pl.loop(0, slots)
    def _(k):
        source = lax.fori_loop(
            0,
            half,
            lambda s, v: v + jnp.where(first_ref[s] == k, ids_ref[other + s], 0),
            jnp.int32(0),
            unroll=True,
        )
        for j in range(own_a):
            xfar[j, k] = xs[source, j]

    @pl.loop(0, half)
    def _(s):
        xlast[s] = xs[ids_ref[other + s], own_a - 1]

    for j in range(own_a - 1):
        by_role(functools.partial(far_copy, j=j))
    pl.when(jnp.logical_not(is_gate))(far_copy("far", own_a - 1).start)

    @pl.when(is_gate)
    def _():
        @pl.loop(0, half)
        def _(n):
            last_copy(lax.rem(n + side * quarter, half)).start()

    @pl.when(is_gate)
    def _():
        for part, kind in enumerate(kinds):
            far_leg_copy(kind).wait_recv()

            @pl.loop(0, half)
            def _(s):
                def store(m, value):
                    lfwd[part, s, m] = value

                pick_legs(s, leg_gate[kind], store)

            lbuf[owner[kind] + lane] = lfwd[part, own]

            @pl.loop(1, half)
            def _(t):
                pass_leg_copy(kind, t).start()

        start_near(1)

    tables(base, True)

    @pl.loop(0, extent)
    def _(b):
        acc[pl.ds(pl.multiple_of(b * extent, extent), extent), :] = jnp.zeros(
            (extent, extent), jnp.float32
        )

    lbuf[me] = lnear[own]
    for c in range(2):
        for j in range(near):
            xall[(c * half + own) * near + j] = xnear[own, c * near + j]

    factors = []
    for d in range(MOST):
        value = weights_ref[jnp.minimum(start_ref[me] + d, diagrams - 1)]
        factors.append(jnp.where(d < counts_ref[me], value, 0.0))

    take(lbuf.at[pl.ds(0, half - 1)], lrecv.at[0])
    take_lanes(lambda lanes: lbuf.at[pl.ds(0, 2 * lanes)], grecv.at[0])

    @pl.loop(0, MOST * LEGS)
    def _(m):
        for v in range(workers):
            low = pl.multiple_of(m * extent, extent) + v * own_rows
            legs[pl.ds(low, own_rows), :] = lbuf[v, m].astype(jnp.float32)

    def leg(m):
        return legs[m * extent : (m + 1) * extent, :]

    firsts = []
    for d in range(MOST):
        firsts.append(leg(LEGS * d).astype(jnp.bfloat16))
        p2s[d * extent : (d + 1) * extent, :] = leg(LEGS * d + 1).astype(jnp.bfloat16)
        p3s[d] = leg(LEGS * d + 2).T.astype(jnp.bfloat16)
    wall = jnp.concatenate(firsts, axis=1)
    width = MOST * size
    at = lax.broadcasted_iota(jnp.int32, (MOST * extent, width), 0)
    for g in range(groups):
        key = key_row(g, side, workers, own_a, slots)
        chosen = jnp.where(at == key, 1.0, 0.0).astype(jnp.bfloat16)
        p1s[g] = jnp.dot(wall, chosen, preferred_element_type=jnp.float32).astype(jnp.bfloat16)

    def forward(kind, j):
        part = kinds.index(kind)

        @pl.when(is_gate)
        def _():
            far_copy(kind, j).wait_recv()

            @pl.loop(0, half)
            def _(s):
                fwd[part, j, s] = gate[kind][j][slot_ref[s]]

            xall[low_of[kind] + j * quarter + lane] = fwd[part, j, own]

            @pl.loop(1, half)
            def _(t):
                pass_copy(kind, j, t).start()

    near_steps, item_steps = size // GROUP, quarter // GROUP
    begin = 2 * near_steps
    main_steps = begin + item_steps * main
    last_steps = item_steps * (len(items) - main)
    last = last_steps * GROUP
    rank = 2 * WIDE + PAD

    def reached(value, limit):
        span = 2 * workers * own_a
        return lax.div(value - limit + span, span)

    def pieces(b, columns, count):
        cols = [
            mid[pl.ds(WIDE * b + h, MOST * count, stride=step), :].astype(jnp.bfloat16)
            for h in range(WIDE)
        ]
        t = jnp.dot(columns, jnp.concatenate(cols, axis=1), preferred_element_type=jnp.float32)
        out = []
        for h in range(WIDE):
            at = pl.ds(pl.multiple_of((WIDE * b + h) * extent, 8), extent)
            out.append((at, t[:, h * extent : (h + 1) * extent] + acc[at, :]))
        return out

    @pl.loop(0, main_steps + last_steps)
    def _(st):
        for f, (kind, j) in enumerate(items[:-1]):
            pl.when(st == when[f])(functools.partial(forward, kind, j))

        for c in range(2):

            @pl.when(st == c * near_steps)
            def _():
                take(xall.at[pl.ds(0, (half - 1) * near)], nrecv.at[c])

        past = reached(st, begin)
        i = lax.div(past * (st - begin), item_steps)
        inside = lax.rem(past * (st - begin), item_steps)
        middle, end = reached(i, early), reached(i, early + own_a)
        part = 1 - middle + end
        j = i - middle * early - end * (own_a - early)
        low = half * own_a + (part * own_a + j) * quarter

        @pl.when(jnp.logical_and(past == 1, inside == 0))
        def _():
            direct = i == len(items) - 1

            @pl.when(direct)
            def _():
                take(xall.at[pl.ds(0, quarter)], frecv.at[part, j])

            @pl.when(jnp.logical_not(direct))
            def _():
                take_lanes(lambda lanes: xall.at[pl.ds(0, lanes)], frecv.at[part, j])

        x_at = (1 - past) * st * GROUP + past * (low + inside * GROUP)
        final = reached(st, main_steps)
        stride = size + final * (last - size)
        start = ((1 - final) * lax.rem(st, near_steps) + final * (st - main_steps)) * GROUP
        both = jnp.concatenate([xall[x_at + n] for n in range(GROUP)], axis=1)
        for d in range(MOST):
            z = jnp.dot(
                p2s[d * extent : (d + 1) * extent, :], both, preferred_element_type=jnp.float32
            ).astype(jnp.bfloat16)
            stacked = jnp.concatenate(
                [z[:, n * extent : (n + 1) * extent] for n in range(GROUP)], axis=0
            )
            y = jnp.dot(stacked, p3s[d], preferred_element_type=jnp.float32) * factors[d]
            for n in range(GROUP):
                at = pl.multiple_of((d * stride + start + n) * step, 8)
                mid[pl.ds(at, extent), :] = y[n * extent : (n + 1) * extent]

        full = jnp.logical_and(st < main_steps, lax.rem(st, near_steps) == near_steps - 1)

        @pl.when(jnp.logical_or(full, st == main_steps - 1))
        def _():
            g = lax.div(st, near_steps)

            @pl.loop(0, extent // WIDE)
            def _(b):
                for at, piece in pieces(b, p1s[g], size):
                    acc[at, :] = piece

    @pl.loop(0, extent // (2 * WIDE))
    def _(b):
        for part in range(2):
            for h, (at, piece) in enumerate(
                pieces(2 * b + part, p1s[groups - 1, :, : MOST * last], last)
            ):
                stage[pl.ds(part * WIDE + h, extent, stride=rank), :] = piece
        at = pl.ds(pl.multiple_of(2 * WIDE * b, 2 * WIDE), 2 * WIDE)
        done = stage[...].reshape(extent, rank, extent)[:, : 2 * WIDE, :]
        o_ref[:, at, :] = done.astype(jnp.bfloat16)

    take(lnear.at[pl.ds(0, half - 1)], lsend.at[0])
    far_leg_copy("far").wait_send()
    take(xnear.at[pl.ds(0, half - 1)], nsend.at[0])
    pl.when(jnp.logical_not(is_gate))(lambda: take(xfar, csend.at[0]))

    @pl.when(is_gate)
    def _():
        take(lfwd.at[:, pl.ds(0, half - 1)], gsend.at[0])
        take(fwd.at[0, :, pl.ds(0, half - 1)], fsend.at[0])
        take(fwd.at[1, pl.ds(0, own_a - 1), pl.ds(0, half - 1)], fsend.at[1])
        take(xfar.at[pl.ds(0, own_a - 1)], csend.at[0])
        take(xlast, dsend.at[0])


def contract(x, perambs, ids, pids, counts, weights, *, workers, slots, number):
    own_a, extent = x.shape[1], x.shape[2]
    own_rows = own_a
    half, quarter = workers // 2, workers // 4
    _, _, size, groups, _, _ = plan(workers, own_a, slots)
    step = extent + PAD
    smem = pl.BlockSpec(memory_space=pltpu.SMEM)
    hbm = pl.BlockSpec(memory_space=pltpu.HBM)
    slab = (extent, extent)
    bf16, f32 = jnp.bfloat16, jnp.float32
    legs = MOST * LEGS
    pieces = (perambs.shape[0], own_rows, extent)
    dma = pltpu.SemaphoreType.DMA
    return pl.pallas_call(
        functools.partial(contract_kernel, workers, slots),
        out_shape=jax.ShapeDtypeStruct((extent, extent, extent), bf16),
        in_specs=[smem, smem, smem, smem, hbm, hbm],
        out_specs=pl.BlockSpec(memory_space=pltpu.VMEM),
        scratch_shapes=[
            pltpu.VMEM(x.shape, bf16),
            pltpu.VMEM(perambs.shape, bf16),
            pltpu.VMEM(pieces, bf16),
            pltpu.VMEM((half, own_a) + slab, bf16),
            pltpu.VMEM((own_a, slots) + slab, bf16),
            pltpu.VMEM((half,) + slab, bf16),
            pltpu.VMEM((half, legs, own_rows, extent), bf16),
            pltpu.VMEM(pieces, bf16),
            pltpu.VMEM(pieces, bf16),
            pltpu.VMEM((2, half, legs, own_rows, extent), bf16),
            pltpu.VMEM((workers * own_a,) + slab, bf16),
            pltpu.VMEM((workers, legs, own_rows, extent), bf16),
            pltpu.VMEM((2, own_a, half) + slab, bf16),
            pltpu.VMEM((legs * extent, extent), f32),
            pltpu.VMEM((groups, extent, MOST * size), bf16),
            pltpu.VMEM((MOST * extent, extent), bf16),
            pltpu.VMEM((MOST,) + slab, bf16),
            pltpu.VMEM((MOST * size * step, extent), f32),
            pltpu.VMEM((extent * extent, extent), f32),
            pltpu.VMEM((extent * (2 * WIDE + PAD), extent), f32),
            pltpu.SMEM((half,), jnp.int32),
            pltpu.SMEM((half,), jnp.int32),
            pltpu.SMEM((half,), jnp.int32),
            pltpu.SMEM((workers,), jnp.int32),
            dma((2,)),
            dma((1,)),
            dma((1,)),
            dma((1,)),
            dma((2,)),
            dma((1,)),
            dma((1,)),
            dma((1,)),
            dma((2,)),
            dma((1,)),
            dma((1,)),
            dma((2, own_a)),
            dma((2,)),
            dma((2, own_a)),
        ]
        + [pltpu.VMEM((slots,) + slab, bf16) for _ in range(2 * own_a - 1)],
        compiler_params=pltpu.CompilerParams(
            vmem_limit_bytes=48 * 1024 * 1024, collective_id=number, has_side_effects=True
        ),
        name=f"contract_{slots}",
    )(ids, pids, counts, weights, x, perambs)


def choose_kernel(caps, ids_ref, o_ref):
    half = ids_ref.shape[0] // 2

    def distinct(low):
        def one(s, count):
            v = ids_ref[low + s]
            seen = lax.fori_loop(
                0,
                half,
                lambda k, m: m + jnp.where(jnp.logical_and(k < s, ids_ref[low + k] == v), 1, 0),
                jnp.int32(0),
                unroll=True,
            )
            return count + jnp.where(seen == 0, 1, 0)

        return lax.fori_loop(0, half, one, jnp.int32(0), unroll=half <= 8)

    most = jnp.maximum(distinct(0), distinct(half))
    which = jnp.int32(0)
    for cap in caps[:-1]:
        which = which + jnp.where(most > cap, 1, 0)
    o_ref[0] = which


def choose(ids, caps):
    smem = pl.BlockSpec(memory_space=pltpu.SMEM)
    return pl.pallas_call(
        functools.partial(choose_kernel, caps),
        out_shape=jax.ShapeDtypeStruct((1,), jnp.int32),
        in_specs=[smem],
        out_specs=smem,
        name="choose",
    )(ids)[0]


def per_device(sources, perambs, source_ids, peramb_ids, sink_counts, weights):
    workers = lax.axis_size("work")
    extent = sources.shape[2]
    own_a = sources.shape[1] // extent
    x = sources.reshape(-1, own_a, extent, extent)
    half = workers // 2
    caps = sorted({-(-half * part // 8) for part in (6, 7, 8)})
    which = choose(source_ids, caps)
    total = lax.switch(
        which,
        [
            functools.partial(contract, workers=workers, slots=cap, number=i)
            for i, cap in enumerate(caps)
        ],
        x,
        perambs,
        source_ids,
        peramb_ids.T,
        sink_counts,
        weights,
    )
    return total.reshape(1, extent * extent, extent)


def solution(mesh):
    return jax.shard_map(
        per_device,
        mesh=mesh,
        in_specs=(P("cfg", "work", None), P("cfg", "work"), P(), P(), P(), P()),
        out_specs=P(("cfg", "work"), None, None),
        check_vma=False,
    )
```
